512 devices in a mesh: tm: 32 (over y, z_hi), gz: 4 (over z_lo, core), row: 4 (over x).
Axes of the slice: x: 4, y: 8, z: 8 (z_hi: 4, z_lo: 2; z = z_hi * 2 + z_lo), core: 2. Of those that a mesh axis runs over, the one named last changes fastest.
Arguments:
- starts: float32 [32, 6, 256, 2048], P('tm', None, 'row', 'gz'), may hold values from -6 to 6
- coarse_map: float32 [32, 36, 64, 512], P('tm', None, 'row', 'gz'), may hold values from -0.2 to 1, as said below
- diffusivity: float32 [6], replicated, may hold values from 0.5 to 1
Outputs:
- next_starts: float32 [32, 6, 256, 2048], P('tm', None, 'row', 'gz')
The draws below stay inside these ranges and needn't reach their ends.
Inputs may be any that keep to these rules, and one draw needn't show every extreme that they name: `coarse_map`: in every coarse cell the absolute values of each row of the matrix sum to at most 0.99; diagonal entries are positive.
All inputs are finite; a program needn't handle non-finite values.
Results may differ from the reference program's by a relative error of at most 0.0001.
Values sent between devices are 32-bit elements; how exact they have to be, the bound alone decides.
No kernel may reach another device: no remote copies, remote signals or barrier semaphores. Data moves between devices by JAX's collectives and lax.ppermute only.
A program may use at most 64 MiB of HBM per device.

```python
import math
import jax
import jax.numpy as jnp
from jax import lax

FIELDS = 6
FSTEPS = 4
TIME_PARTITIONS = 32
NR = 256
NZ = 2048
NRC = 64
NZC = 512


def draw_coarse_map(key, part):
    random_key_list = jax.random.split(jax.random.fold_in(key, 17), 6)
    slow_count = 3
    order = jax.random.permutation(random_key_list[0], 6)
    sluggish_indicator = (order < slow_count)[None, :, None, None]
    base_slow = jax.random.uniform(random_key_list[1], (TIME_PARTITIONS, 6, 1, 1), jnp.float32, 0.96, 0.99)
    base_fast = jax.random.uniform(random_key_list[2], (TIME_PARTITIONS, 6, 1, 1), jnp.float32, 0.25, 0.55)
    cell_factor = jax.random.uniform(random_key_list[3], (TIME_PARTITIONS, 6, NRC, NZC), jnp.float32, 0.985, 1.0)
    surge_partitions = jax.random.randint(random_key_list[4], (2,), 0, TIME_PARTITIONS)
    surge_indicator = jnp.any(jnp.arange(TIME_PARTITIONS)[:, None] == surge_partitions[None, :], axis=1)[:, None, None, None]
    diagonal_entries = jnp.where(sluggish_indicator, base_slow, base_fast) * cell_factor
    diagonal_entries = diagonal_entries * jnp.where(jnp.logical_and(surge_indicator, sluggish_indicator), 0.7, 1.0)
    offset = jax.random.uniform(random_key_list[5], (TIME_PARTITIONS, 6, 6, NRC, NZC), jnp.float32, -1.0, 1.0)
    offset = offset * ((0.99 - diagonal_entries) / 5.0)[:, :, None]
    identity_matrix = jnp.eye(6, dtype=jnp.float32)[None, :, :, None, None]
    matrix = offset * (1.0 - identity_matrix) + identity_matrix * diagonal_entries[:, :, None]
    return matrix.reshape(TIME_PARTITIONS, 36, NRC, NZC)


def block_levels(own_key, dims, shards, low, top_value):
    def one(axis_at, blocks):
        steps = jax.random.uniform(jax.random.fold_in(jax.random.fold_in(own_key, 6), axis_at), (blocks,), jnp.float32, low / len(shards), top_value / len(shards))
        return jnp.repeat(jnp.exp(steps), dims[axis_at] // blocks).reshape((-1,) + (1,) * (len(dims) - axis_at - 1))

    loudness = one(*shards[0])
    for cut in shards[1:]:
        loudness = loudness * one(*cut)
    return loudness


def bell_draw(rng, shape, width, reach, cuts=(), kind=jnp.bfloat16):
    array = jax.random.normal(rng, shape, jnp.float32) * width
    if len(cuts) > 0:
        array = block_levels(rng, shape, cuts, -0.22, 0.18) * array
    return jnp.clip(array, min=-reach, max=reach).astype(kind)


def setup_inputs(seed: int = 0) -> dict:
    keys = jax.random.split(jax.random.key(seed), 4)
    starts = bell_draw(keys[0], (TIME_PARTITIONS, FIELDS, NR, NZ), 1.0, 6.0, ((0, 32), (2, 4), (3, 4)), jnp.float32)
    coarse_map = draw_coarse_map(jax.random.fold_in(keys[3], 71), 0)
    diffusivity = jnp.clip(jnp.exp(jax.random.uniform(keys[2], (FIELDS,), jnp.float32, math.log(0.5), math.log(1.0))), 0.5, 1.0)
    return {"starts": starts, "coarse_map": coarse_map, "diffusivity": diffusivity}


time_step = 0.24


def fine_step(padded, row_start, diffusivity):
    center = padded[:, 1:-1, 1:-1]
    height_rows = center.shape[1]
    speed = 0.25 * jnp.tanh(padded[1])
    east_cell = padded[:, 1:-1, 2:]
    west_cell = padded[:, 1:-1, :-2]
    north_cell = padded[:, 2:, 1:-1]
    south_cell = padded[:, :-2, 1:-1]
    speed_mid = speed[1:-1, 1:-1]
    eastward_flux = 0.25 * (speed_mid + speed[1:-1, 2:]) * (center + east_cell)
    flux_west = 0.25 * (speed_mid + speed[1:-1, :-2]) * (center + west_cell)
    radius = (row_start + jnp.arange(height_rows, dtype=jnp.int32)).astype(jnp.float32)[:, None]
    radial = ((radius + 1.0) * (north_cell - center) - radius * (center - south_cell)) / (radius + 0.5)
    spread_rate = diffusivity[:, None, None]
    change = spread_rate * (radial + east_cell - 2.0 * center + west_cell) - (eastward_flux - flux_west)
    return center + time_step * change


def restrict(field):
    count, height_rows, width_cols = field.shape
    return field.reshape(count, height_rows // 4, 4, width_cols // 4, 4).mean(axis=(2, 4))


def prolong(field):
    return jnp.repeat(jnp.repeat(field, 4, axis=1), 4, axis=2)


def apply_map(matrix, vector):
    return jnp.sum(matrix * vector[None], axis=1)


def reference(starts, coarse_map, diffusivity):
    later_starts = jnp.concatenate([starts[1:], jnp.zeros_like(starts[:1])], axis=0)

    def slice_turn(carry, inputs):
        start_state, later_state, matrix_flat = inputs
        matrix = matrix_flat.reshape(6, 6, matrix_flat.shape[1], matrix_flat.shape[2])

        def one_step(turn_index, state):
            padded = jnp.pad(state, ((0, 0), (1, 1), (1, 1)))
            return fine_step(padded, 0, diffusivity)

        fine_state = lax.fori_loop(0, FSTEPS, one_step, start_state)
        jump = restrict(fine_state) - restrict(later_state)
        mapped = apply_map(matrix, carry)
        result = fine_state + prolong(mapped)
        return mapped + jump, result

    carry_zero = jnp.zeros((FIELDS, NRC, NZC), jnp.float32)
    last_carry, outputs = lax.scan(slice_turn, carry_zero, (starts, later_starts, coarse_map))
    return outputs
```

```python
import functools

import jax
import jax.numpy as jnp
from jax import lax
from jax.experimental import pallas as pl
from jax.experimental.pallas import tpu as pltpu
from jax.sharding import PartitionSpec as P

FSTEPS = 4
STEP = 0.24
FACE = 0.24 * 0.25 * 0.25
F32 = jnp.float32
TOP = 16
BUF = 96
PARAMS = pltpu.CompilerParams(vmem_limit_bytes=24 << 20)
VMEM = pl.BlockSpec(memory_space=pltpu.VMEM)
SMEM = pl.BlockSpec(memory_space=pltpu.SMEM)


def lanes(shape):
    return lax.broadcasted_iota(jnp.int32, shape, len(shape) - 1)


def columns_kernel(first_ref, last_ref, above0_ref, above3_ref, below0_ref, below3_ref, right_ref, left_ref):
    def packed(refs, shift):
        for rows, ref in refs:
            lane = lanes(ref.shape[1:])
            total = jnp.zeros(ref.shape[1:], F32)
            for f in range(6):
                moved = pltpu.roll(ref[f], (4 * f + shift) % 128, 1)
                total = jnp.where((lane >= 4 * f) & (lane < 4 * f + 4), moved, total)
            yield rows, total

    for rows, total in packed(((0, last_ref), (64, below3_ref), (68, above3_ref)), 4):
        right_ref[rows : rows + total.shape[0], :] = total
    for rows, total in packed(((0, first_ref), (64, below0_ref), (68, above0_ref)), 0):
        left_ref[rows : rows + total.shape[0], :] = total


def pack_columns(state, above, below):
    whole = lambda t: pl.BlockSpec((6, 64, 128), lambda i: (0, 0, t))
    strip = lambda t: pl.BlockSpec((6, 4, 128), lambda i: (0, 0, t))
    out = jax.ShapeDtypeStruct((72, 128), F32)
    spec = pl.BlockSpec((72, 128), lambda i: (0, 0))
    return pl.pallas_call(
        columns_kernel,
        grid=(1,),
        out_shape=(out, out),
        in_specs=[whole(0), whole(3), strip(0), strip(3), strip(0), strip(3)],
        out_specs=(spec, spec),
        compiler_params=PARAMS,
        name="columns",
    )(state, state, above, above, below, below)


def restricted(buffer, slot, sums):
    for f in range(6):
        for t in range(4):
            total = buffer[slot, f, t, pl.ds(TOP, 16, stride=4), :]
            for k in range(1, 4):
                total = total + buffer[slot, f, t, pl.ds(TOP + k, 16, stride=4), :]
            sums[16 * f : 16 * f + 16, 128 * t : 128 * t + 128] = total
    cell = lax.broadcasted_iota(jnp.int32, (512, 128), 0)
    coarse = lax.broadcasted_iota(jnp.int32, (512, 128), 1)
    average = jnp.where(cell // 4 == coarse, F32(1.0 / 16.0), F32(0.0))
    return jnp.dot(sums[...], average, precision=lax.Precision.HIGHEST, preferred_element_type=F32)


def put_pair(packed_ref, k, low, high):
    left = lanes(low.shape) < 64
    even = jnp.where(left, low, pltpu.roll(high, 64, 1))
    odd = jnp.where(left, pltpu.roll(low, 64, 1), high)
    packed_ref[pl.ds(k, 16, stride=48), :] = even
    packed_ref[pl.ds(24 + k, 16, stride=48), :] = odd


def fine_kernel(place_ref, nu_ref, state_ref, above_ref, below_ref, from_left_ref, from_right_ref, map_ref,
                fine_ref, packed_ref, buffer, face, weights, sums):
    row, column = place_ref[0], place_ref[1]
    lane = lanes((8, 128))
    for f in range(6):
        for t in range(4):
            cut = slice(128 * t, 128 * t + 128)
            buffer[0, f, t, TOP : TOP + 64, :] = state_ref[f, :, cut]
            buffer[0, f, t, TOP - 4 : TOP, :] = above_ref[f, :, cut]
            buffer[0, f, t, TOP + 64 : TOP + 68, :] = below_ref[f, :, cut]
        for source, target, count in ((0, TOP, 64), (64, TOP + 64, 4), (68, TOP - 4, 4)):
            at = lanes((count, 128))
            right = pltpu.roll(from_right_ref[source : source + count, :], (128 - 4 * f) % 128, 1)
            left = pltpu.roll(from_left_ref[source : source + count, :], 124 - 4 * f, 1)
            halo = jnp.where(at < 4, right, jnp.where(at >= 124, left, F32(0.0)))
            buffer[0, f, 4, target : target + count, :] = halo
    cell = lax.broadcasted_iota(jnp.int32, (BUF, 128), 0) - TOP + row * 64
    radius = cell.astype(F32)
    weights[0] = (radius + 1.0) / (radius + 0.5)
    weights[1] = radius / (radius + 0.5)
    for f in range(6):
        for j in range(3):
            put_pair(packed_ref, 3 * f + j, map_ref[6 * f + j], map_ref[6 * f + j + 3])
    means = restricted(buffer, 0, sums)
    for j in range(3):
        put_pair(packed_ref, 21 + j, means[16 * j : 16 * j + 16], means[16 * j + 48 : 16 * j + 64])

    low, high = jnp.where(column < 3, 64, 0), jnp.where(column > 0, 64, 128)
    inside_side = (lane < low) | (lane >= high)

    def east(values):
        moved = [pltpu.roll(v, 127, 1) for v in values]
        n = len(moved)
        return [jnp.where(lane < 127, moved[t], moved[(t + 1) % n]) for t in range(n)]

    def west(values):
        moved = [pltpu.roll(v, 1, 1) for v in values]
        n = len(moved)
        return [jnp.where(lane > 0, moved[t], moved[(t - 1) % n]) for t in range(n)]

    def one_step(step, last):
        now, later = step % 2, (step + 1) % 2
        tiles = range(2, 10) if last else range(1, 11)
        for i in tiles:
            rows = pl.ds(8 * i, 8)
            speed = [FACE * jnp.tanh(buffer[now, 1, t, rows, :]) for t in range(5)]
            for t, (a, b) in enumerate(zip(speed, east(speed))):
                face[t, rows, :] = a + b

        def one_field(f, nothing):
            k = STEP * nu_ref[f]
            keep = 1.0 - 2.0 * k
            for i in tiles:
                rows = pl.ds(8 * i, 8)
                center = [buffer[now, f, t, rows, :] for t in range(5)]
                flux = []
                for t, (c, e) in enumerate(zip(center, east(center))):
                    g = face[t, rows, :]
                    flux.append(e * (k - g) - c * (k + g))
                back = west(flux)
                up, down = weights[0, rows, :], weights[1, rows, :]
                for t in range(4 if last else 5):
                    north = buffer[now, f, t, pl.ds(8 * i + 1, 8), :]
                    south = buffer[now, f, t, pl.ds(8 * i - 1, 8), :]
                    new = keep * center[t] + k * (up * north + down * south) + (flux[t] - back[t])
                    if i == 1:
                        new = jnp.where(row > 0, new, F32(0.0))
                    if i == 10:
                        new = jnp.where(row < 3, new, F32(0.0))
                    if t == 4:
                        new = jnp.where(inside_side, new, F32(0.0))
                    buffer[later, f, t, rows, :] = new
                    if last:
                        fine_ref[f, 8 * i - TOP : 8 * i - TOP + 8, 128 * t : 128 * t + 128] = new
            return nothing

        lax.fori_loop(0, 6, one_field, 0)

    for step in range(FSTEPS):
        one_step(step, step == FSTEPS - 1)
    means = restricted(buffer, FSTEPS % 2, sums)
    for j in range(3):
        put_pair(packed_ref, 18 + j, means[16 * j : 16 * j + 16], means[16 * j + 48 : 16 * j + 64])


def fine(place, diffusivity, state, above, below, from_left, from_right, coarse_map):
    return pl.pallas_call(
        fine_kernel,
        out_shape=(jax.ShapeDtypeStruct((6, 64, 512), F32), jax.ShapeDtypeStruct((768, 128), F32)),
        in_specs=[SMEM, SMEM] + [VMEM] * 6,
        out_specs=(VMEM, VMEM),
        scratch_shapes=[
            pltpu.VMEM((2, 6, 5, BUF, 128), F32),
            pltpu.VMEM((5, BUF, 128), F32),
            pltpu.VMEM((2, BUF, 128), F32),
            pltpu.VMEM((96, 512), F32),
        ],
        compiler_params=PARAMS,
        name="fine",
    )(place, diffusivity, state, above, below, from_left, from_right, coarse_map)


def scan_kernel(slices, packed_ref, mapped_ref):
    left = lanes((1, 128)) < 64
    carry = [jnp.zeros((1, 128), F32)] * 3
    for n in range(slices):
        base = 24 * n
        line = lambda k: packed_ref[pl.ds(base + k, 1), :]
        sums = []
        for f in range(6):
            sums.append(line(3 * f) * carry[0] + line(3 * f + 1) * carry[1] + line(3 * f + 2) * carry[2])
        mapped = []
        for j in range(3):
            own = jnp.where(left, sums[j], sums[j + 3])
            other = jnp.where(left, sums[j + 3], sums[j])
            mapped.append(own + pltpu.roll(other, 64, 1))
            mapped_ref[pl.ds(4 * n + j, 1), :] = mapped[j]
        if n < slices - 1:
            carry = [
                mapped[j] + (line(18 + j) - packed_ref[pl.ds(base + 24 + 21 + j, 1), :]) for j in range(3)
            ]


def scanned(packed, slices):
    return pl.pallas_call(
        functools.partial(scan_kernel, slices),
        out_shape=jax.ShapeDtypeStruct((4 * slices, 128), F32),
        in_specs=[VMEM],
        out_specs=VMEM,
        compiler_params=PARAMS,
        name="scan",
    )(packed)


def final_kernel(fine_ref, mapped_ref, out_ref, wide):
    left = lanes((16, 128)) < 64
    upper = lax.broadcasted_iota(jnp.int32, (8, 128), 0) < 4
    for f in range(6):
        j = f % 3
        even = mapped_ref[pl.ds(j, 16, stride=8), :]
        odd = mapped_ref[pl.ds(4 + j, 16, stride=8), :]
        if f < 3:
            cells = jnp.where(left, even, pltpu.roll(odd, 64, 1))
        else:
            cells = jnp.where(left, pltpu.roll(even, 64, 1), odd)
        for t in range(4):
            source = 32 * t + lanes((16, 128)) // 4
            wide[f, t] = jnp.take_along_axis(cells, source, axis=1)
    for f in range(6):
        for t in range(4):
            cut = slice(128 * t, 128 * t + 128)
            for q in range(8):
                first = jnp.broadcast_to(wide[f, t, pl.ds(2 * q, 1), :], (8, 128))
                second = jnp.broadcast_to(wide[f, t, pl.ds(2 * q + 1, 1), :], (8, 128))
                rows = slice(8 * q, 8 * q + 8)
                out_ref[f, rows, cut] = fine_ref[f, rows, cut] + jnp.where(upper, first, second)


def final(fine_state, mapped):
    return pl.pallas_call(
        final_kernel,
        out_shape=jax.ShapeDtypeStruct((6, 64, 512), F32),
        in_specs=[VMEM, VMEM],
        out_specs=VMEM,
        scratch_shapes=[pltpu.VMEM((6, 4, 16, 128), F32)],
        compiler_params=PARAMS,
        name="final",
    )(fine_state, mapped)


def swapped(first, last, axis):
    size = lax.axis_size(axis)
    up = [(i, i + 1) for i in range(size - 1)]
    down = [(i + 1, i) for i in range(size - 1)]
    return lax.ppermute(last, axis, up), lax.ppermute(first, axis, down)


def local(starts, coarse_map, diffusivity):
    state, entries = starts[0], coarse_map[0]
    slices = lax.axis_size("tm")
    place = jnp.stack([lax.axis_index("row"), lax.axis_index("gz")]).astype(jnp.int32)
    above, below = swapped(state[:, :4, :], state[:, 60:, :], "row")
    to_right, to_left = pack_columns(state, above, below)
    from_left, from_right = swapped(to_left, to_right, "gz")
    fine_state, packed = fine(place, diffusivity, state, above, below, from_left, from_right, entries)
    packed = lax.all_to_all(packed, "tm", 0, 0, tiled=True)
    mapped = scanned(packed, slices)
    mapped = lax.all_to_all(mapped, "tm", 0, 0, tiled=True)
    return final(fine_state, mapped)[None]


def solution(mesh):
    placed = (P("tm", None, "row", "gz"), P("tm", None, "row", "gz"), P())
    return jax.shard_map(
        local, mesh=mesh, in_specs=placed, out_specs=P("tm", None, "row", "gz"), check_vma=False
    )
```

```python
import functools

import jax
import jax.numpy as jnp
from jax import lax
from jax.experimental import pallas as pl
from jax.experimental.pallas import tpu as pltpu
from jax.sharding import PartitionSpec as P

FSTEPS = 4
STEP = 0.24
FACE = 0.24 * 0.25 * 0.25
F32, BF16 = jnp.float32, jnp.bfloat16
TOP = 16
BUF = 96
PARAMS = pltpu.CompilerParams(vmem_limit_bytes=24 << 20)
VMEM = pl.BlockSpec(memory_space=pltpu.VMEM)
SMEM = pl.BlockSpec(memory_space=pltpu.SMEM)
HBM = pl.BlockSpec(memory_space=pltpu.HBM)


def lanes(shape):
    return lax.broadcasted_iota(jnp.int32, shape, len(shape) - 1)


def put_pair(packed_ref, k, low, high):
    left = lanes(low.shape) < 64
    packed_ref[pl.ds(k, 16, stride=48), :] = jnp.where(left, low, pltpu.roll(high, 64, 1))
    packed_ref[pl.ds(24 + k, 16, stride=48), :] = jnp.where(left, pltpu.roll(low, 64, 1), high)


def split_dot(x, matrix, transposed=False):
    high = x.astype(BF16)
    low = (x - high.astype(F32)).astype(BF16)
    dims = (((1,), (1 if transposed else 0,)), ((), ()))
    dot = lambda part: lax.dot_general(part, matrix, dims, preferred_element_type=F32)
    return dot(high) + dot(low)


PLACES = [(0, q, q) for q in range(4)] + [(1, q, 4 + q) for q in range(2)] + [(2, q, 1) for q in range(4)]


def moved(x, shift):
    shift = shift % 128
    return pltpu.roll(x, shift, 1) if shift else x


def messages(column, count):
    lane = lanes((count, 128))
    right, left = jnp.zeros((count, 128), F32), jnp.zeros((count, 128), F32)
    for tile, q, f in PLACES:
        at = 32 * q + 4 * tile
        right = jnp.where((lane >= at) & (lane < at + 4), moved(column(f, 3), at + 4), right)
        at = 32 * q + 24 - 4 * tile
        left = jnp.where((lane >= at) & (lane < at + 4), moved(column(f, 0), at), left)
    return right, left


def put_strips(strips_ref, rows, column, count):
    lane = lanes((count, 128))
    for tile in range(3):
        total = jnp.zeros((count, 128), F32)
        for other, q, f in PLACES:
            if other == tile:
                at = 32 * q
                total = jnp.where((lane >= at + 4) & (lane < at + 12), moved(column(f, 0), at + 4), total)
                total = jnp.where((lane >= at + 16) & (lane < at + 24), moved(column(f, 3), at + 24), total)
        strips_ref[tile, rows : rows + count, :] = total


def prep_kernel(place_ref, nu_ref, starts_ref, map_ref, cells_ref, packed_ref, pair_ref, cross_ref, strips_ref,
                consts_ref, weights_ref, order_ref, spread_ref, state, entries, sems):
    row, column = place_ref[0], place_ref[1]
    state_copy = pltpu.make_async_copy(starts_ref, state, sems.at[0])
    map_copy = pltpu.make_async_copy(map_ref, entries, sems.at[1])
    state_copy.start()
    map_copy.start()
    for t in range(4):
        z = lax.broadcasted_iota(jnp.int32, (128, 512), 0) + 128 * t
        place = lax.broadcasted_iota(jnp.int32, (128, 512), 1)
        order_ref[128 * t : 128 * t + 128, :] = jnp.where(128 * (z % 4) + z // 4 == place, F32(1), F32(0)).astype(BF16)
    lane = lax.broadcasted_iota(jnp.int32, (256, 384), 0)
    target = lax.broadcasted_iota(jnp.int32, (256, 384), 1)
    field, at = lane // 32, lane % 32
    base = jnp.where(field < 3, 128 * field, 128 * (field - 3) + 64)
    to = jnp.where((at >= 4) & (at < 8), base, jnp.where((at >= 20) & (at < 24), base + 63, -1))
    to = jnp.where(field < 6, to, -1)
    spread_ref[...] = jnp.where(to == target, F32(1.0 / 16.0), F32(0.0)).astype(BF16)
    line, lane = lax.broadcasted_iota(jnp.int32, (8, 128), 0), lanes((8, 128))
    flag = lambda condition: jnp.where(condition, F32(1.0), F32(0.0))
    group, at = lane // 32, lane % 32
    low, high = jnp.where(column > 0, 0, 4), jnp.where(column < 3, 32, 24)
    rates = lambda fields: functools.reduce(
        lambda a, q: jnp.where(group == q, STEP * nu_ref[fields[q]], a), range(4), jnp.zeros((8, 128), F32)
    )
    values = [flag(row % 2 == 1), flag(column % 2 == 1), flag(row > 0), flag(row < 3)]
    values += [flag((at >= low) & (at < high)), rates((0, 1, 2, 3)), rates((4, 5, 5, 5)), rates((1, 1, 1, 1))]
    total = jnp.zeros((8, 128), F32)
    for r, value in enumerate(values):
        total = jnp.where(line == r, value, total)
    consts_ref[...] = total
    radius = (lax.broadcasted_iota(jnp.int32, (BUF, 128), 0) - TOP + row * 64).astype(F32)
    weights_ref[0] = (radius + 1.0) / (radius + 0.5)
    weights_ref[1] = radius / (radius + 0.5)

    state_copy.wait()
    piece = lambda f, t: state[f, :, 128 * t : 128 * t + 128]
    odd = column % 2 == 1
    right, left = messages(piece, 64)
    pair_ref[0:64, :] = jnp.where(odd, left, right)
    cross_ref[0:64, :] = jnp.where(odd, right, left)
    put_strips(strips_ref, 0, piece, 64)
    ordered = split_dot(state[...].reshape(384, 512), order_ref[...])
    for f in range(6):
        for k in range(4):
            cells_ref[f, k] = ordered[64 * f : 64 * f + 64, 128 * k : 128 * k + 128]
    put_means(packed_ref, 21, lambda f, k, r: cells_ref[f, k, pl.ds(r, 16, stride=4), :], False)
    map_copy.wait()
    for f in range(6):
        for j in range(3):
            put_pair(packed_ref, 3 * f + j, entries[6 * f + j], entries[6 * f + j + 3])


def put_means(packed_ref, at, load, inner):
    means = []
    for f in range(6):
        total = jnp.zeros((16, 128), F32)
        for k in range(4):
            total = total + ((load(f, k, 0) + load(f, k, 1)) + (load(f, k, 2) + load(f, k, 3)))
        if inner:
            lane = lanes((16, 128))
            total = jnp.where((lane > 0) & (lane < 127), total, F32(0.0))
        means.append(total * F32(1.0 / 16.0))
    for j in range(3):
        put_pair(packed_ref, at + j, means[j], means[j + 3])


def prep(place, diffusivity, state, coarse_map):
    shape = lambda *dims: jax.ShapeDtypeStruct(dims, F32)
    return pl.pallas_call(
        prep_kernel,
        out_shape=(
            shape(6, 4, 64, 128),
            shape(768, 128),
            shape(72, 128),
            shape(72, 128),
            shape(3, 72, 128),
            shape(8, 128),
            shape(2, BUF, 128),
            jax.ShapeDtypeStruct((512, 512), BF16),
            jax.ShapeDtypeStruct((256, 384), BF16),
        ),
        in_specs=[SMEM, SMEM, HBM, HBM],
        out_specs=(VMEM,) * 9,
        scratch_shapes=[
            pltpu.VMEM((6, 64, 512), F32),
            pltpu.VMEM((36, 16, 128), F32),
            pltpu.SemaphoreType.DMA((2,)),
        ],
        compiler_params=PARAMS,
        cost_estimate=pl.CostEstimate(flops=4_000_000, bytes_accessed=2_000_000, transcendentals=0),
        name="prep",
    )(place, diffusivity, state, coarse_map)


def const(consts_ref, r):
    return consts_ref[pl.ds(r, 1), :]


def strips_above_below(consts_ref, pair_rows_ref, cross_rows_ref):
    odd = jnp.broadcast_to(const(consts_ref, 0), (4, 128)) > 0.5
    pick = lambda a, b: lambda f, t: jnp.where(
        odd, a[f, :, 128 * t : 128 * t + 128], b[f, :, 128 * t : 128 * t + 128]
    )
    return pick(pair_rows_ref, cross_rows_ref), pick(cross_rows_ref, pair_rows_ref)


def corners_kernel(consts_ref, pair_rows_ref, cross_rows_ref, pair_in, cross_in, pair_ref, cross_ref):
    del pair_in, cross_in
    odd = jnp.broadcast_to(const(consts_ref, 1), (4, 128)) > 0.5
    above, below = strips_above_below(consts_ref, pair_rows_ref, cross_rows_ref)
    for at, piece in ((64, below), (68, above)):
        right, left = messages(piece, 4)
        pair_ref[at : at + 4, :] = jnp.where(odd, left, right)
        cross_ref[at : at + 4, :] = jnp.where(odd, right, left)


def corners(consts, pair_rows, cross_rows, pair_columns, cross_columns):
    out = jax.ShapeDtypeStruct((72, 128), F32)
    return pl.pallas_call(
        corners_kernel,
        out_shape=(out, out),
        in_specs=[VMEM] * 5,
        out_specs=(VMEM, VMEM),
        input_output_aliases={3: 0, 4: 1},
        compiler_params=PARAMS,
        name="corners",
    )(consts, pair_rows, cross_rows, pair_columns, cross_columns)


def middle_kernel(nu_ref, consts_ref, weights_ref, order_ref, cells_ref, pair_rows_ref, cross_rows_ref, packed_in,
                  strips_in, fine_ref, packed_ref, strips_ref, buffer, face, halo, flat):
    del packed_in, strips_in
    above, below = strips_above_below(consts_ref, pair_rows_ref, cross_rows_ref)
    for f in range(6):
        for t in range(4):
            halo[8 * f : 8 * f + 4, 128 * t : 128 * t + 128] = above(f, t)
            halo[8 * f + 4 : 8 * f + 8, 128 * t : 128 * t + 128] = below(f, t)
    put_strips(strips_ref, 64, below, 4)
    put_strips(strips_ref, 68, above, 4)
    ordered = split_dot(halo[...], order_ref[...])
    for f in range(6):
        for k in range(4):
            buffer[0, f, k, TOP : TOP + 64, :] = cells_ref[f, k]
            piece = ordered[8 * f : 8 * f + 8, 128 * k : 128 * k + 128]
            buffer[0, f, k, TOP - 4 : TOP, :] = piece[0:4]
            buffer[0, f, k, TOP + 64 : TOP + 68, :] = piece[4:8]
    has_above = jnp.broadcast_to(const(consts_ref, 2), (8, 128)) > 0.5
    has_below = jnp.broadcast_to(const(consts_ref, 3), (8, 128)) > 0.5

    def step_cells(now, later, tiles, last):
        for i in tiles:
            rows = pl.ds(8 * i, 8)
            speed = [FACE * jnp.tanh(buffer[now, 1, k, rows, :]) for k in range(4)]
            face[0, rows, :] = speed[0] + pltpu.roll(speed[3], 1, 1)
            for k in range(4):
                face[k + 1, rows, :] = speed[k] + (speed[k + 1] if k < 3 else pltpu.roll(speed[0], 127, 1))
            for k in range(4):
                face[5 + k, rows, :] = face[k, rows, :] - face[k + 1, rows, :]
        for f in range(6):
            rate = STEP * nu_ref[f]
            keep = 1.0 - 4.0 * rate
            for i in tiles:
                rows = pl.ds(8 * i, 8)
                center = [buffer[now, f, k, rows, :] for k in range(4)]
                east = center[1:] + [pltpu.roll(center[0], 127, 1)]
                west = [pltpu.roll(center[3], 1, 1)] + center[:3]
                up, down = rate * weights_ref[0, rows, :], rate * weights_ref[1, rows, :]
                for k in range(4):
                    north = buffer[now, f, k, pl.ds(8 * i + 1, 8), :]
                    south = buffer[now, f, k, pl.ds(8 * i - 1, 8), :]
                    new = (up * north + down * south) + (
                        (east[k] * (rate - face[k + 1, rows, :]) + west[k] * (rate + face[k, rows, :]))
                        + center[k] * (keep + face[5 + k, rows, :])
                    )
                    if i == 1:
                        new = jnp.where(has_above, new, F32(0.0))
                    if i == 10:
                        new = jnp.where(has_below, new, F32(0.0))
                    buffer[later, f, k, rows, :] = new
                    if last:
                        at = 64 * f + 8 * i - TOP
                        flat[at : at + 8, 128 * k : 128 * k + 128] = new

    for step in range(FSTEPS):
        last = step == FSTEPS - 1
        step_cells(step % 2, (step + 1) % 2, range(2, 10) if last else range(1, 11), last)
    slot = FSTEPS % 2
    put_means(packed_ref, 18, lambda f, k, r: buffer[slot, f, k, pl.ds(TOP + r, 16, stride=4), :], True)
    fine_ref[...] = split_dot(flat[...], order_ref[...], transposed=True).reshape(6, 64, 512)


def middle(diffusivity, consts, weights, order, cells, pair_rows, cross_rows, packed, strips):
    return pl.pallas_call(
        middle_kernel,
        out_shape=(
            jax.ShapeDtypeStruct((6, 64, 512), F32),
            jax.ShapeDtypeStruct((768, 128), F32),
            jax.ShapeDtypeStruct((3, 72, 128), F32),
        ),
        in_specs=[SMEM] + [VMEM] * 8,
        out_specs=(VMEM,) * 3,
        scratch_shapes=[
            pltpu.VMEM((2, 6, 4, BUF, 128), F32),
            pltpu.VMEM((9, BUF, 128), F32),
            pltpu.VMEM((48, 512), F32),
            pltpu.VMEM((384, 512), F32),
        ],
        input_output_aliases={7: 1, 8: 2},
        compiler_params=PARAMS,
        cost_estimate=pl.CostEstimate(flops=20_000_000, bytes_accessed=4_000_000, transcendentals=200_000),
        name="middle",
    )(diffusivity, consts, weights, order, cells, pair_rows, cross_rows, packed, strips)


def sides_kernel(consts_ref, weights_ref, spread_ref, strips_ref, pair_ref, cross_ref, packed_in,
                 edge_ref, packed_ref, buffer, face):
    full = lambda r, count=8: jnp.broadcast_to(const(consts_ref, r), (count, 128))
    for source, target, count in ((0, TOP, 64), (64, TOP + 64, 4), (68, TOP - 4, 4)):
        at = lanes((count, 128)) % 32
        odd = full(1, count) > 0.5
        pair, cross = pair_ref[source : source + count, :], cross_ref[source : source + count, :]
        from_left, from_right = jnp.where(odd, pair, cross), jnp.where(odd, cross, pair)
        for tile in range(3):
            value = jnp.where(at < 4, moved(from_left, -4 * tile), strips_ref[tile, source : source + count, :])
            value = jnp.where((at >= 24) & (at < 28), moved(from_right, 4 * tile), value)
            buffer[0, tile, target : target + count, :] = value
    has_above, has_below, inside = full(2) > 0.5, full(3) > 0.5, full(4) > 0.5
    rates = [full(5 + tile) for tile in range(3)]
    keeps = [1.0 - 4.0 * rate for rate in rates]
    for step in range(FSTEPS):
        now, later = step % 2, (step + 1) % 2
        last = step == FSTEPS - 1
        tiles = range(2, 10) if last else range(1, 11)
        for i in tiles:
            rows = pl.ds(8 * i, 8)
            speed = FACE * jnp.tanh(buffer[now, 2, rows, :])
            face[0, rows, :] = speed + pltpu.roll(speed, 127, 1)
            face[1, rows, :] = speed + pltpu.roll(speed, 1, 1)
        for i in tiles:
            rows = pl.ds(8 * i, 8)
            up, down = weights_ref[0, rows, :], weights_ref[1, rows, :]
            fe, fw = face[0, rows, :], face[1, rows, :]
            for tile in range(2 if last else 3):
                rate = rates[tile]
                center = buffer[now, tile, rows, :]
                north = buffer[now, tile, pl.ds(8 * i + 1, 8), :]
                south = buffer[now, tile, pl.ds(8 * i - 1, 8), :]
                new = rate * (up * north + down * south) + (
                    (pltpu.roll(center, 127, 1) * (rate - fe) + pltpu.roll(center, 1, 1) * (rate + fw))
                    + center * (keeps[tile] + (fw - fe))
                )
                if i == 1:
                    new = jnp.where(has_above, new, F32(0.0))
                if i == 10:
                    new = jnp.where(has_below, new, F32(0.0))
                new = jnp.where(inside, new, F32(0.0))
                buffer[later, tile, rows, :] = new
                if last:
                    edge_ref[tile, 8 * i - TOP : 8 * i - TOP + 8, :] = new
    slot = FSTEPS % 2
    sums = []
    for tile in range(2):
        load = lambda r: buffer[slot, tile, pl.ds(TOP + r, 16, stride=4), :]
        sums.append((load(0) + load(1)) + (load(2) + load(3)))
    own = split_dot(jnp.concatenate(sums, axis=1), spread_ref[...])
    left = lanes((16, 128)) % 64 == 0
    for j in range(3):
        piece = own[:, 128 * j : 128 * j + 128]
        even, odd = pl.ds(18 + j, 16, stride=48), pl.ds(42 + j, 16, stride=48)
        packed_ref[even, :] = packed_in[even, :] + jnp.where(left, piece, F32(0.0))
        packed_ref[odd, :] = packed_in[odd, :] + jnp.where(left, F32(0.0), piece)


def sides(consts, weights, spread, strips, pair_columns, cross_columns, packed):
    return pl.pallas_call(
        sides_kernel,
        out_shape=(jax.ShapeDtypeStruct((2, 64, 128), F32), jax.ShapeDtypeStruct((768, 128), F32)),
        in_specs=[VMEM] * 7,
        out_specs=(VMEM, VMEM),
        scratch_shapes=[pltpu.VMEM((2, 3, BUF, 128), F32), pltpu.VMEM((2, BUF, 128), F32)],
        input_output_aliases={6: 1},
        compiler_params=PARAMS,
        name="sides",
    )(consts, weights, spread, strips, pair_columns, cross_columns, packed)


def scan_kernel(slices, packed_ref, mapped_ref, other, rows):
    other[...] = pltpu.roll(packed_ref[...], 64, 1)
    carry = [jnp.zeros((1, 128), F32)] * 6
    for n in range(slices):
        base = 24 * n
        line = lambda k, half: (other if half else packed_ref)[pl.ds(base + k, 1), :]
        mapped = []
        for f in range(6):
            terms = [line(3 * f + g % 3, g >= 3) * carry[g] for g in range(6)]
            total = (terms[0] + terms[1]) + (terms[2] + terms[3]) + (terms[4] + terms[5])
            rows[f, pl.ds(n, 1), :] = total
            mapped.append(total)
        if n < slices - 1:
            carry = [mapped[f] + (line(18 + f % 3, f >= 3) - line(45 + f % 3, f >= 3)) for f in range(6)]
    left = lanes((slices, 128)) < 64
    for j in range(3):
        mapped_ref[pl.ds(j, slices, stride=4), :] = jnp.where(left, rows[j], pltpu.roll(rows[j + 3], 64, 1))


def scanned(packed, slices):
    return pl.pallas_call(
        functools.partial(scan_kernel, slices),
        out_shape=jax.ShapeDtypeStruct((4 * slices, 128), F32),
        in_specs=[VMEM],
        out_specs=VMEM,
        scratch_shapes=[pltpu.VMEM((24 * slices, 128), F32), pltpu.VMEM((6, slices, 128), F32)],
        compiler_params=PARAMS,
        name="scan",
    )(packed)


def final_kernel(fine_ref, edge_ref, mapped_ref, out_ref, wide, done, sems):
    left = lanes((16, 128)) < 64
    upper = lax.broadcasted_iota(jnp.int32, (8, 128), 0) < 4
    lane = lanes((8, 128))
    for f in range(6):
        j = f % 3
        even = mapped_ref[pl.ds(j, 16, stride=8), :]
        odd = mapped_ref[pl.ds(4 + j, 16, stride=8), :]
        if f < 3:
            cells = jnp.where(left, even, pltpu.roll(odd, 64, 1))
        else:
            cells = jnp.where(left, pltpu.roll(even, 64, 1), odd)
        for t in range(4):
            source = 32 * t + lanes((16, 128)) // 4
            wide[f, t] = jnp.take_along_axis(cells, source, axis=1)
    copies = []
    for f in range(6):
        tile, base = f // 4, 32 * (f % 4)
        for t in range(4):
            cut = slice(128 * t, 128 * t + 128)
            for q in range(8):
                first = jnp.broadcast_to(wide[f, t, pl.ds(2 * q, 1), :], (8, 128))
                second = jnp.broadcast_to(wide[f, t, pl.ds(2 * q + 1, 1), :], (8, 128))
                rows = slice(8 * q, 8 * q + 8)
                own = fine_ref[f, rows, cut]
                if t == 0:
                    own = jnp.where(lane < 4, moved(edge_ref[tile, rows, :], -(base + 4)), own)
                if t == 3:
                    own = jnp.where(lane >= 124, moved(edge_ref[tile, rows, :], 104 - base), own)
                done[f, rows, cut] = own + jnp.where(upper, first, second)
        copies.append(pltpu.make_async_copy(done.at[f], out_ref.at[f], sems.at[f]))
        copies[f].start()
    for copy in copies:
        copy.wait()


def final(fine_state, edge, mapped):
    return pl.pallas_call(
        final_kernel,
        out_shape=jax.ShapeDtypeStruct((6, 64, 512), F32),
        in_specs=[VMEM] * 3,
        out_specs=HBM,
        scratch_shapes=[
            pltpu.VMEM((6, 4, 16, 128), F32),
            pltpu.VMEM((6, 64, 512), F32),
            pltpu.SemaphoreType.DMA((6,)),
        ],
        compiler_params=PARAMS,
        name="final",
    )(fine_state, edge, mapped)


def swapped(pair, cross, axis):
    size = lax.axis_size(axis)
    couples = lambda first: [(i, i + 1) for i in range(first, size - 1, 2)]
    both = lambda links: links + [(b, a) for a, b in links]
    return lax.ppermute(pair, axis, both(couples(0))), lax.ppermute(cross, axis, both(couples(1)))


def local(starts, coarse_map, diffusivity):
    state = pltpu.with_memory_space_constraint(starts[0], pltpu.HBM)
    entries = pltpu.with_memory_space_constraint(coarse_map[0], pltpu.HBM)
    slices = lax.axis_size("tm")
    row = lax.axis_index("row")
    place = jnp.stack([row, lax.axis_index("gz")]).astype(jnp.int32)
    first, last = starts[0, :, :4, :], starts[0, :, 60:, :]
    odd = row % 2 == 1
    pair_rows, cross_rows = swapped(jnp.where(odd, first, last), jnp.where(odd, last, first), "row")
    cells, packed, pair_columns, cross_columns, strips, consts, weights, order, spread = prep(
        place, diffusivity, state, entries
    )
    pair_columns, cross_columns = corners(consts, pair_rows, cross_rows, pair_columns, cross_columns)
    pair_columns, cross_columns = swapped(pair_columns, cross_columns, "gz")
    fine_state, packed, strips = middle(
        diffusivity, consts, weights, order, cells, pair_rows, cross_rows, packed, strips
    )
    edge, packed = sides(consts, weights, spread, strips, pair_columns, cross_columns, packed)
    packed = lax.all_to_all(packed, "tm", 0, 0, tiled=True)
    mapped = scanned(packed, slices)
    mapped = lax.all_to_all(mapped, "tm", 0, 0, tiled=True)
    return final(fine_state, edge, mapped)[None]


def solution(mesh):
    placed = (P("tm", None, "row", "gz"), P("tm", None, "row", "gz"), P())
    return jax.shard_map(
        local, mesh=mesh, in_specs=placed, out_specs=P("tm", None, "row", "gz"), check_vma=False
    )
```

```python
import functools

import jax
import jax.numpy as jnp
from jax import lax
from jax.experimental import pallas as pl
from jax.experimental.pallas import tpu as pltpu
from jax.sharding import PartitionSpec as P

FSTEPS = 4
STEP = 0.24
FACE = 0.24 * 0.25 * 0.25
F32, BF16 = jnp.float32, jnp.bfloat16
TOP = 16
BUF = 96
PARAMS = pltpu.CompilerParams(vmem_limit_bytes=24 << 20)
VMEM = pl.BlockSpec(memory_space=pltpu.VMEM)
SMEM = pl.BlockSpec(memory_space=pltpu.SMEM)
HBM = pl.BlockSpec(memory_space=pltpu.HBM)


def lanes(shape):
    return lax.broadcasted_iota(jnp.int32, shape, len(shape) - 1)


def put_pair(packed_ref, k, low, high):
    left = lanes(low.shape) < 64
    packed_ref[pl.ds(k, 16, stride=48), :] = jnp.where(left, low, pltpu.roll(high, 64, 1))
    packed_ref[pl.ds(24 + k, 16, stride=48), :] = jnp.where(left, pltpu.roll(low, 64, 1), high)


def split_dot(x, matrix, transposed=False):
    high = x.astype(BF16)
    low = (x - high.astype(F32)).astype(BF16)
    dims = (((1,), (1 if transposed else 0,)), ((), ()))
    dot = lambda part: lax.dot_general(part, matrix, dims, preferred_element_type=F32)
    return dot(high) + dot(low)


PLACES = [(0, q, q) for q in range(4)] + [(1, q, 4 + q) for q in range(2)] + [(2, q, 1) for q in range(4)]


def moved(x, shift):
    shift = shift % 128
    return pltpu.roll(x, shift, 1) if shift else x


def messages(column, count):
    lane = lanes((count, 128))
    right, left = jnp.zeros((count, 128), F32), jnp.zeros((count, 128), F32)
    for tile, q, f in PLACES:
        at = 32 * q + 4 * tile
        right = jnp.where((lane >= at) & (lane < at + 4), moved(column(f, 3), at + 4), right)
        at = 32 * q + 24 - 4 * tile
        left = jnp.where((lane >= at) & (lane < at + 4), moved(column(f, 0), at), left)
    return right, left


def put_strips(strips_ref, rows, column, count):
    lane = lanes((count, 128))
    for tile in range(3):
        total = jnp.zeros((count, 128), F32)
        for other, q, f in PLACES:
            if other == tile:
                at = 32 * q
                total = jnp.where((lane >= at + 4) & (lane < at + 12), moved(column(f, 0), at + 4), total)
                total = jnp.where((lane >= at + 16) & (lane < at + 24), moved(column(f, 3), at + 24), total)
        strips_ref[tile, rows : rows + count, :] = total


def load_kernel(nu_hbm, starts_ref, state_ref, pair_ref, cross_ref, consts_ref, weights_ref, order_ref, spread_ref, nu_ref, sems):
    outer = [pl.ds(0, 8), pl.ds(56, 8), pl.ds(8, 48)]
    copies = [pltpu.make_async_copy(starts_ref.at[:, r, :], state_ref.at[:, r, :], sems.at[i]) for i, r in enumerate(outer)]
    copies.append(pltpu.make_async_copy(nu_hbm, nu_ref, sems.at[3]))
    for copy in copies:
        copy.start()
    row, column = lax.axis_index("row"), lax.axis_index("gz")
    for t in range(4):
        z = lax.broadcasted_iota(jnp.int32, (128, 512), 0) + 128 * t
        place = lax.broadcasted_iota(jnp.int32, (128, 512), 1)
        order_ref[128 * t : 128 * t + 128, :] = jnp.where(128 * (z % 4) + z // 4 == place, F32(1), F32(0)).astype(BF16)
    lane = lax.broadcasted_iota(jnp.int32, (256, 384), 0)
    target = lax.broadcasted_iota(jnp.int32, (256, 384), 1)
    field, at = lane // 32, lane % 32
    base = jnp.where(field < 3, 128 * field, 128 * (field - 3) + 64)
    to = jnp.where((at >= 4) & (at < 8), base, jnp.where((at >= 20) & (at < 24), base + 63, -1))
    to = jnp.where(field < 6, to, -1)
    spread_ref[...] = jnp.where(to == target, F32(1.0 / 16.0), F32(0.0)).astype(BF16)
    radius = (lax.broadcasted_iota(jnp.int32, (BUF, 128), 0) - TOP + row * 64).astype(F32)
    weights_ref[0] = (radius + 1.0) / (radius + 0.5)
    weights_ref[1] = radius / (radius + 0.5)
    copies[3].wait()
    line, lane = lax.broadcasted_iota(jnp.int32, (16, 128), 0), lanes((16, 128))
    flag = lambda condition: jnp.where(condition, F32(1.0), F32(0.0))
    group, at = lane // 32, lane % 32
    low, high = jnp.where(column > 0, 0, 4), jnp.where(column < 3, 32, 24)
    rates = lambda fields: functools.reduce(
        lambda a, q: jnp.where(group == q, STEP * nu_ref[fields[q]], a), range(4), jnp.zeros((16, 128), F32)
    )
    values = [flag(row % 2 == 1), flag(column % 2 == 1), flag(row > 0), flag(row < 3)]
    values += [flag((at >= low) & (at < high)), rates((0, 1, 2, 3)), rates((4, 5, 5, 5)), rates((1, 1, 1, 1))]
    values += [rates((f, f, f, f)) for f in range(6)]
    total = jnp.zeros((16, 128), F32)
    for r, value in enumerate(values):
        total = jnp.where(line == r, value, total)
    consts_ref[...] = total
    copies[0].wait()
    copies[1].wait()
    odd = row % 2 == 1
    for f in range(6):
        first, last = state_ref[f, 0:4, :], state_ref[f, 60:64, :]
        pair_ref[f] = jnp.where(odd, first, last)
        cross_ref[f] = jnp.where(odd, last, first)
    copies[2].wait()


def load(diffusivity, state):
    shape = lambda *dims: jax.ShapeDtypeStruct(dims, F32)
    return pl.pallas_call(
        load_kernel,
        out_shape=(
            shape(6, 64, 512),
            shape(6, 4, 512),
            shape(6, 4, 512),
            shape(16, 128),
            shape(2, BUF, 128),
            jax.ShapeDtypeStruct((512, 512), BF16),
            jax.ShapeDtypeStruct((256, 384), BF16),
        ),
        in_specs=[HBM, HBM],
        out_specs=(VMEM,) * 7,
        scratch_shapes=[pltpu.SMEM((6,), F32), pltpu.SemaphoreType.DMA((4,))],
        compiler_params=PARAMS,
        name="load",
    )(diffusivity, state)


def prep_kernel(consts_ref, order_ref, state_ref, map_ref, cells_ref, packed_ref, pair_ref, cross_ref, strips_ref, entries, sem):
    map_copy = pltpu.make_async_copy(map_ref, entries, sem)
    map_copy.start()
    piece = lambda f, t: state_ref[f, :, 128 * t : 128 * t + 128]
    odd = jnp.broadcast_to(const(consts_ref, 1), (64, 128)) > 0.5
    right, left = messages(piece, 64)
    pair_ref[0:64, :] = jnp.where(odd, left, right)
    cross_ref[0:64, :] = jnp.where(odd, right, left)
    put_strips(strips_ref, 0, piece, 64)
    ordered = split_dot(state_ref[...].reshape(384, 512), order_ref[...])
    for f in range(6):
        for k in range(4):
            cells_ref[f, k] = ordered[64 * f : 64 * f + 64, 128 * k : 128 * k + 128]
    put_means(packed_ref, 21, lambda f, k, r: cells_ref[f, k, pl.ds(r, 16, stride=4), :], False)
    map_copy.wait()
    for f in range(6):
        for j in range(3):
            put_pair(packed_ref, 3 * f + j, entries[6 * f + j], entries[6 * f + j + 3])


def put_means(packed_ref, at, load, inner):
    means = []
    for f in range(6):
        total = jnp.zeros((16, 128), F32)
        for k in range(4):
            total = total + ((load(f, k, 0) + load(f, k, 1)) + (load(f, k, 2) + load(f, k, 3)))
        if inner:
            lane = lanes((16, 128))
            total = jnp.where((lane > 0) & (lane < 127), total, F32(0.0))
        means.append(total * F32(1.0 / 16.0))
    for j in range(3):
        put_pair(packed_ref, at + j, means[j], means[j + 3])


def prep(consts, order, state, coarse_map):
    shape = lambda *dims: jax.ShapeDtypeStruct(dims, F32)
    return pl.pallas_call(
        prep_kernel,
        out_shape=(shape(6, 4, 64, 128), shape(768, 128), shape(72, 128), shape(72, 128), shape(3, 72, 128)),
        in_specs=[VMEM, VMEM, VMEM, HBM],
        out_specs=(VMEM,) * 5,
        scratch_shapes=[pltpu.VMEM((36, 16, 128), F32), pltpu.SemaphoreType.DMA(())],
        compiler_params=PARAMS,
        cost_estimate=pl.CostEstimate(flops=4_000_000, bytes_accessed=2_000_000, transcendentals=0),
        name="prep",
    )(consts, order, state, coarse_map)


def const(consts_ref, r):
    return consts_ref[pl.ds(r, 1), :]


def strips_above_below(consts_ref, pair_rows_ref, cross_rows_ref):
    odd = jnp.broadcast_to(const(consts_ref, 0), (4, 128)) > 0.5
    pick = lambda a, b: lambda f, t: jnp.where(
        odd, a[f, :, 128 * t : 128 * t + 128], b[f, :, 128 * t : 128 * t + 128]
    )
    return pick(pair_rows_ref, cross_rows_ref), pick(cross_rows_ref, pair_rows_ref)


def corners_kernel(consts_ref, pair_rows_ref, cross_rows_ref, pair_in, cross_in, pair_ref, cross_ref):
    del pair_in, cross_in
    odd = jnp.broadcast_to(const(consts_ref, 1), (4, 128)) > 0.5
    above, below = strips_above_below(consts_ref, pair_rows_ref, cross_rows_ref)
    for at, piece in ((64, below), (68, above)):
        right, left = messages(piece, 4)
        pair_ref[at : at + 4, :] = jnp.where(odd, left, right)
        cross_ref[at : at + 4, :] = jnp.where(odd, right, left)


def corners(consts, pair_rows, cross_rows, pair_columns, cross_columns):
    out = jax.ShapeDtypeStruct((72, 128), F32)
    return pl.pallas_call(
        corners_kernel,
        out_shape=(out, out),
        in_specs=[VMEM] * 5,
        out_specs=(VMEM, VMEM),
        input_output_aliases={3: 0, 4: 1},
        compiler_params=PARAMS,
        name="corners",
    )(consts, pair_rows, cross_rows, pair_columns, cross_columns)


def middle_kernel(consts_ref, weights_ref, order_ref, cells_ref, pair_rows_ref, cross_rows_ref, packed_in,
                  strips_in, fine_ref, packed_ref, strips_ref, buffer, face, halo, flat):
    del packed_in, strips_in
    above, below = strips_above_below(consts_ref, pair_rows_ref, cross_rows_ref)
    for f in range(6):
        for t in range(4):
            halo[8 * f : 8 * f + 4, 128 * t : 128 * t + 128] = above(f, t)
            halo[8 * f + 4 : 8 * f + 8, 128 * t : 128 * t + 128] = below(f, t)
    put_strips(strips_ref, 64, below, 4)
    put_strips(strips_ref, 68, above, 4)
    ordered = split_dot(halo[...], order_ref[...])
    for f in range(6):
        for k in range(4):
            buffer[0, f, k, TOP : TOP + 64, :] = cells_ref[f, k]
            piece = ordered[8 * f : 8 * f + 8, 128 * k : 128 * k + 128]
            buffer[0, f, k, TOP - 4 : TOP, :] = piece[0:4]
            buffer[0, f, k, TOP + 64 : TOP + 68, :] = piece[4:8]
    has_above = jnp.broadcast_to(const(consts_ref, 2), (8, 128)) > 0.5
    has_below = jnp.broadcast_to(const(consts_ref, 3), (8, 128)) > 0.5

    def step_cells(now, later, tiles, last):
        for i in tiles:
            rows = pl.ds(8 * i, 8)
            speed = [FACE * jnp.tanh(buffer[now, 1, k, rows, :]) for k in range(4)]
            face[0, rows, :] = speed[0] + pltpu.roll(speed[3], 1, 1)
            for k in range(4):
                face[k + 1, rows, :] = speed[k] + (speed[k + 1] if k < 3 else pltpu.roll(speed[0], 127, 1))
            for k in range(4):
                face[5 + k, rows, :] = face[k, rows, :] - face[k + 1, rows, :]
        for f in range(6):
            rate = jnp.broadcast_to(const(consts_ref, 8 + f), (8, 128))
            keep = 1.0 - 4.0 * rate
            for i in tiles:
                rows = pl.ds(8 * i, 8)
                center = [buffer[now, f, k, rows, :] for k in range(4)]
                east = center[1:] + [pltpu.roll(center[0], 127, 1)]
                west = [pltpu.roll(center[3], 1, 1)] + center[:3]
                up, down = rate * weights_ref[0, rows, :], rate * weights_ref[1, rows, :]
                for k in range(4):
                    north = buffer[now, f, k, pl.ds(8 * i + 1, 8), :]
                    south = buffer[now, f, k, pl.ds(8 * i - 1, 8), :]
                    new = (up * north + down * south) + (
                        (east[k] * (rate - face[k + 1, rows, :]) + west[k] * (rate + face[k, rows, :]))
                        + center[k] * (keep + face[5 + k, rows, :])
                    )
                    if i == 1:
                        new = jnp.where(has_above, new, F32(0.0))
                    if i == 10:
                        new = jnp.where(has_below, new, F32(0.0))
                    buffer[later, f, k, rows, :] = new
                    if last:
                        at = 64 * f + 8 * i - TOP
                        flat[at : at + 8, 128 * k : 128 * k + 128] = new

    for step in range(FSTEPS):
        last = step == FSTEPS - 1
        step_cells(step % 2, (step + 1) % 2, range(2, 10) if last else range(1, 11), last)
    slot = FSTEPS % 2
    put_means(packed_ref, 18, lambda f, k, r: buffer[slot, f, k, pl.ds(TOP + r, 16, stride=4), :], True)
    fine_ref[...] = split_dot(flat[...], order_ref[...], transposed=True).reshape(6, 64, 512)


def middle(consts, weights, order, cells, pair_rows, cross_rows, packed, strips):
    return pl.pallas_call(
        middle_kernel,
        out_shape=(
            jax.ShapeDtypeStruct((6, 64, 512), F32),
            jax.ShapeDtypeStruct((768, 128), F32),
            jax.ShapeDtypeStruct((3, 72, 128), F32),
        ),
        in_specs=[VMEM] * 8,
        out_specs=(VMEM,) * 3,
        scratch_shapes=[
            pltpu.VMEM((2, 6, 4, BUF, 128), F32),
            pltpu.VMEM((9, BUF, 128), F32),
            pltpu.VMEM((48, 512), F32),
            pltpu.VMEM((384, 512), F32),
        ],
        input_output_aliases={6: 1, 7: 2},
        compiler_params=PARAMS,
        cost_estimate=pl.CostEstimate(flops=20_000_000, bytes_accessed=4_000_000, transcendentals=200_000),
        name="middle",
    )(consts, weights, order, cells, pair_rows, cross_rows, packed, strips)


def sides_kernel(consts_ref, weights_ref, spread_ref, strips_ref, pair_ref, cross_ref, packed_in,
                 edge_ref, packed_ref, buffer, face):
    full = lambda r, count=8: jnp.broadcast_to(const(consts_ref, r), (count, 128))
    for source, target, count in ((0, TOP, 64), (64, TOP + 64, 4), (68, TOP - 4, 4)):
        at = lanes((count, 128)) % 32
        odd = full(1, count) > 0.5
        pair, cross = pair_ref[source : source + count, :], cross_ref[source : source + count, :]
        from_left, from_right = jnp.where(odd, pair, cross), jnp.where(odd, cross, pair)
        for tile in range(3):
            value = jnp.where(at < 4, moved(from_left, -4 * tile), strips_ref[tile, source : source + count, :])
            value = jnp.where((at >= 24) & (at < 28), moved(from_right, 4 * tile), value)
            buffer[0, tile, target : target + count, :] = value
    has_above, has_below, inside = full(2) > 0.5, full(3) > 0.5, full(4) > 0.5
    rates = [full(5 + tile) for tile in range(3)]
    keeps = [1.0 - 4.0 * rate for rate in rates]
    for step in range(FSTEPS):
        now, later = step % 2, (step + 1) % 2
        last = step == FSTEPS - 1
        tiles = range(2, 10) if last else range(1, 11)
        for i in tiles:
            rows = pl.ds(8 * i, 8)
            speed = FACE * jnp.tanh(buffer[now, 2, rows, :])
            face[0, rows, :] = speed + pltpu.roll(speed, 127, 1)
            face[1, rows, :] = speed + pltpu.roll(speed, 1, 1)
        for i in tiles:
            rows = pl.ds(8 * i, 8)
            up, down = weights_ref[0, rows, :], weights_ref[1, rows, :]
            fe, fw = face[0, rows, :], face[1, rows, :]
            for tile in range(2 if last else 3):
                rate = rates[tile]
                center = buffer[now, tile, rows, :]
                north = buffer[now, tile, pl.ds(8 * i + 1, 8), :]
                south = buffer[now, tile, pl.ds(8 * i - 1, 8), :]
                new = rate * (up * north + down * south) + (
                    (pltpu.roll(center, 127, 1) * (rate - fe) + pltpu.roll(center, 1, 1) * (rate + fw))
                    + center * (keeps[tile] + (fw - fe))
                )
                if i == 1:
                    new = jnp.where(has_above, new, F32(0.0))
                if i == 10:
                    new = jnp.where(has_below, new, F32(0.0))
                new = jnp.where(inside, new, F32(0.0))
                buffer[later, tile, rows, :] = new
                if last:
                    edge_ref[tile, 8 * i - TOP : 8 * i - TOP + 8, :] = new
    slot = FSTEPS % 2
    sums = []
    for tile in range(2):
        load = lambda r: buffer[slot, tile, pl.ds(TOP + r, 16, stride=4), :]
        sums.append((load(0) + load(1)) + (load(2) + load(3)))
    own = split_dot(jnp.concatenate(sums, axis=1), spread_ref[...])
    left = lanes((16, 128)) % 64 == 0
    for j in range(3):
        piece = own[:, 128 * j : 128 * j + 128]
        even, odd = pl.ds(18 + j, 16, stride=48), pl.ds(42 + j, 16, stride=48)
        packed_ref[even, :] = packed_in[even, :] + jnp.where(left, piece, F32(0.0))
        packed_ref[odd, :] = packed_in[odd, :] + jnp.where(left, F32(0.0), piece)


def sides(consts, weights, spread, strips, pair_columns, cross_columns, packed):
    return pl.pallas_call(
        sides_kernel,
        out_shape=(jax.ShapeDtypeStruct((2, 64, 128), F32), jax.ShapeDtypeStruct((768, 128), F32)),
        in_specs=[VMEM] * 7,
        out_specs=(VMEM, VMEM),
        scratch_shapes=[pltpu.VMEM((2, 3, BUF, 128), F32), pltpu.VMEM((2, BUF, 128), F32)],
        input_output_aliases={6: 1},
        compiler_params=PARAMS,
        name="sides",
    )(consts, weights, spread, strips, pair_columns, cross_columns, packed)


def scan_kernel(slices, packed_ref, mapped_ref, other, rows):
    other[...] = pltpu.roll(packed_ref[...], 64, 1)
    carry = [jnp.zeros((1, 128), F32)] * 6
    for n in range(slices):
        base = 24 * n
        line = lambda k, half: (other if half else packed_ref)[pl.ds(base + k, 1), :]
        mapped = []
        for f in range(6):
            terms = [line(3 * f + g % 3, g >= 3) * carry[g] for g in range(6)]
            total = (terms[0] + terms[1]) + (terms[2] + terms[3]) + (terms[4] + terms[5])
            rows[f, pl.ds(n, 1), :] = total
            mapped.append(total)
        if n < slices - 1:
            carry = [mapped[f] + (line(18 + f % 3, f >= 3) - line(45 + f % 3, f >= 3)) for f in range(6)]
    left = lanes((slices, 128)) < 64
    for j in range(3):
        mapped_ref[pl.ds(j, slices, stride=4), :] = jnp.where(left, rows[j], pltpu.roll(rows[j + 3], 64, 1))


def scanned(packed, slices):
    return pl.pallas_call(
        functools.partial(scan_kernel, slices),
        out_shape=jax.ShapeDtypeStruct((4 * slices, 128), F32),
        in_specs=[VMEM],
        out_specs=VMEM,
        scratch_shapes=[pltpu.VMEM((24 * slices, 128), F32), pltpu.VMEM((6, slices, 128), F32)],
        compiler_params=PARAMS,
        name="scan",
    )(packed)


def final_kernel(fine_ref, edge_ref, mapped_ref, out_ref, wide, done, sems):
    left = lanes((16, 128)) < 64
    upper = lax.broadcasted_iota(jnp.int32, (8, 128), 0) < 4
    lane = lanes((8, 128))
    for f in range(6):
        j = f % 3
        even = mapped_ref[pl.ds(j, 16, stride=8), :]
        odd = mapped_ref[pl.ds(4 + j, 16, stride=8), :]
        if f < 3:
            cells = jnp.where(left, even, pltpu.roll(odd, 64, 1))
        else:
            cells = jnp.where(left, pltpu.roll(even, 64, 1), odd)
        for t in range(4):
            source = 32 * t + lanes((16, 128)) // 4
            wide[f, t] = jnp.take_along_axis(cells, source, axis=1)
    copies = []
    for f in range(6):
        tile, base = f // 4, 32 * (f % 4)
        for t in range(4):
            cut = slice(128 * t, 128 * t + 128)
            for q in range(8):
                first = jnp.broadcast_to(wide[f, t, pl.ds(2 * q, 1), :], (8, 128))
                second = jnp.broadcast_to(wide[f, t, pl.ds(2 * q + 1, 1), :], (8, 128))
                rows = slice(8 * q, 8 * q + 8)
                own = fine_ref[f, rows, cut]
                if t == 0:
                    own = jnp.where(lane < 4, moved(edge_ref[tile, rows, :], -(base + 4)), own)
                if t == 3:
                    own = jnp.where(lane >= 124, moved(edge_ref[tile, rows, :], 104 - base), own)
                done[f, rows, cut] = own + jnp.where(upper, first, second)
        copies.append(pltpu.make_async_copy(done.at[f], out_ref.at[f], sems.at[f]))
        copies[f].start()
    for copy in copies:
        copy.wait()


def final(fine_state, edge, mapped):
    return pl.pallas_call(
        final_kernel,
        out_shape=jax.ShapeDtypeStruct((6, 64, 512), F32),
        in_specs=[VMEM] * 3,
        out_specs=HBM,
        scratch_shapes=[
            pltpu.VMEM((6, 4, 16, 128), F32),
            pltpu.VMEM((6, 64, 512), F32),
            pltpu.SemaphoreType.DMA((6,)),
        ],
        compiler_params=PARAMS,
        name="final",
    )(fine_state, edge, mapped)


def swapped(pair, cross, axis):
    size = lax.axis_size(axis)
    couples = lambda first: [(i, i + 1) for i in range(first, size - 1, 2)]
    both = lambda links: links + [(b, a) for a, b in links]
    return lax.ppermute(pair, axis, both(couples(0))), lax.ppermute(cross, axis, both(couples(1)))


def local(starts, coarse_map, diffusivity):
    in_hbm = lambda x: pltpu.with_memory_space_constraint(x, pltpu.HBM)
    slices = lax.axis_size("tm")
    state, pair_rows, cross_rows, consts, weights, order, spread = load(in_hbm(diffusivity), in_hbm(starts[0]))
    pair_rows, cross_rows = swapped(pair_rows, cross_rows, "row")
    cells, packed, pair_columns, cross_columns, strips = prep(consts, order, state, in_hbm(coarse_map[0]))
    pair_columns, cross_columns = corners(consts, pair_rows, cross_rows, pair_columns, cross_columns)
    pair_columns, cross_columns = swapped(pair_columns, cross_columns, "gz")
    fine_state, packed, strips = middle(consts, weights, order, cells, pair_rows, cross_rows, packed, strips)
    edge, packed = sides(consts, weights, spread, strips, pair_columns, cross_columns, packed)
    packed = lax.all_to_all(packed, "tm", 0, 0, tiled=True)
    mapped = scanned(packed, slices)
    mapped = lax.all_to_all(mapped, "tm", 0, 0, tiled=True)
    return final(fine_state, edge, mapped)[None]


def solution(mesh):
    placed = (P("tm", None, "row", "gz"), P("tm", None, "row", "gz"), P())
    return jax.shard_map(
        local, mesh=mesh, in_specs=placed, out_specs=P("tm", None, "row", "gz"), check_vma=False
    )
```

```python
import functools

import jax
import jax.numpy as jnp
from jax import lax
from jax.experimental import pallas as pl
from jax.experimental.pallas import tpu as pltpu
from jax.sharding import PartitionSpec as P

FSTEPS = 4
STEP = 0.24
FACE = 0.24 * 0.25 * 0.25
F32, BF16 = jnp.float32, jnp.bfloat16
TOP = 8
BUF = 88
PARAMS = pltpu.CompilerParams(vmem_limit_bytes=24 << 20)
VMEM = pl.BlockSpec(memory_space=pltpu.VMEM)
SMEM = pl.BlockSpec(memory_space=pltpu.SMEM)
HBM = pl.BlockSpec(memory_space=pltpu.HBM)


def lanes(shape):
    return lax.broadcasted_iota(jnp.int32, shape, len(shape) - 1)


SLOT, BACK = 21, 3


def put_pair(packed_ref, k, low, high, height=SLOT):
    left = lanes(low.shape) < 64
    packed_ref[pl.ds(k, 16, stride=2 * height), :] = jnp.where(left, low, pltpu.roll(high, 64, 1))
    packed_ref[pl.ds(height + k, 16, stride=2 * height), :] = jnp.where(left, pltpu.roll(low, 64, 1), high)


def split_dot(x, matrix, transposed=False):
    high = x.astype(BF16)
    low = (x - high.astype(F32)).astype(BF16)
    dims = (((1,), (1 if transposed else 0,)), ((), ()))
    dot = lambda part: lax.dot_general(part, matrix, dims, preferred_element_type=F32)
    return dot(high) + dot(low)


PLACES = [(0, q, q) for q in range(4)] + [(1, q, 4 + q) for q in range(2)] + [(2, q, 1) for q in range(4)]


def moved(x, shift):
    shift = shift % 128
    return pltpu.roll(x, shift, 1) if shift else x


def messages(column, count):
    lane = lanes((count, 128))
    right, left = jnp.zeros((count, 128), F32), jnp.zeros((count, 128), F32)
    for tile, q, f in PLACES:
        at = 32 * q + 4 * tile
        right = jnp.where((lane >= at) & (lane < at + 4), moved(column(f, 3), at + 4), right)
        at = 32 * q + 24 - 4 * tile
        left = jnp.where((lane >= at) & (lane < at + 4), moved(column(f, 0), at), left)
    return right, left


def put_strips(strips_ref, rows, column, count):
    lane = lanes((count, 128))
    for tile in range(3):
        total = jnp.zeros((count, 128), F32)
        for other, q, f in PLACES:
            if other == tile:
                at = 32 * q
                total = jnp.where((lane >= at + 4) & (lane < at + 12), moved(column(f, 0), at + 4), total)
                total = jnp.where((lane >= at + 16) & (lane < at + 24), moved(column(f, 3), at + 24), total)
        strips_ref[tile, rows : rows + count, :] = total


def load_kernel(nu_hbm, starts_ref, map_ref, state_ref, entries_ref, pair_ref, cross_ref, consts_ref, weights_ref, order_ref,
                spread_ref, nu_ref, sems):
    outer = [pl.ds(0, 8), pl.ds(56, 8), pl.ds(8, 48)]
    copies = [pltpu.make_async_copy(starts_ref.at[:, r, :], state_ref.at[:, r, :], sems.at[i]) for i, r in enumerate(outer)]
    copies.append(pltpu.make_async_copy(nu_hbm, nu_ref, sems.at[3]))
    copies.append(pltpu.make_async_copy(map_ref, entries_ref, sems.at[4]))
    for copy in copies:
        copy.start()
    row, column = lax.axis_index("row"), lax.axis_index("gz")
    for t in range(4):
        z = lax.broadcasted_iota(jnp.int32, (128, 512), 0) + 128 * t
        place = lax.broadcasted_iota(jnp.int32, (128, 512), 1)
        order_ref[128 * t : 128 * t + 128, :] = jnp.where(128 * (z % 4) + z // 4 == place, F32(1), F32(0)).astype(BF16)
    lane = lax.broadcasted_iota(jnp.int32, (256, 384), 0)
    target = lax.broadcasted_iota(jnp.int32, (256, 384), 1)
    field, at = lane // 32, lane % 32
    base = jnp.where(field < 3, 128 * field, 128 * (field - 3) + 64)
    to = jnp.where((at >= 4) & (at < 8), base, jnp.where((at >= 20) & (at < 24), base + 63, -1))
    to = jnp.where(field < 6, to, -1)
    spread_ref[...] = jnp.where(to == target, F32(1.0 / 16.0), F32(0.0)).astype(BF16)
    line = lax.broadcasted_iota(jnp.int32, (BUF, 128), 0)
    radius = (jnp.where(line >= TOP + 68, line - (TOP + 72), line - TOP) + row * 64).astype(F32)
    weights_ref[0] = (radius + 1.0) / (radius + 0.5)
    weights_ref[1] = radius / (radius + 0.5)
    copies[3].wait()
    line, lane = lax.broadcasted_iota(jnp.int32, (16, 128), 0), lanes((16, 128))
    flag = lambda condition: jnp.where(condition, F32(1.0), F32(0.0))
    group, at = lane // 32, lane % 32
    low, high = jnp.where(column > 0, 0, 4), jnp.where(column < 3, 32, 24)
    rates = lambda fields: functools.reduce(
        lambda a, q: jnp.where(group == q, STEP * nu_ref[fields[q]], a), range(4), jnp.zeros((16, 128), F32)
    )
    values = [flag(row % 2 == 1), flag(column % 2 == 1), flag(row > 0), flag(row < 3)]
    values += [flag((at >= low) & (at < high)), rates((0, 1, 2, 3)), rates((4, 5, 5, 5)), rates((1, 1, 1, 1))]
    values += [rates((f, f, f, f)) for f in range(6)]
    values += [flag(lax.axis_index("tm") > 0)]
    total = jnp.zeros((16, 128), F32)
    for r, value in enumerate(values):
        total = jnp.where(line == r, value, total)
    consts_ref[...] = total
    copies[0].wait()
    copies[1].wait()
    odd = row % 2 == 1
    for f in range(6):
        first, last = state_ref[f, 0:4, :], state_ref[f, 60:64, :]
        pair_ref[f] = jnp.where(odd, first, last)
        cross_ref[f] = jnp.where(odd, last, first)
    copies[2].wait()
    copies[4].wait()


def load(diffusivity, state, coarse_map):
    shape = lambda *dims: jax.ShapeDtypeStruct(dims, F32)
    return pl.pallas_call(
        load_kernel,
        out_shape=(
            shape(6, 64, 512),
            shape(36, 16, 128),
            shape(6, 4, 512),
            shape(6, 4, 512),
            shape(16, 128),
            shape(2, BUF, 128),
            jax.ShapeDtypeStruct((512, 512), BF16),
            jax.ShapeDtypeStruct((256, 384), BF16),
        ),
        in_specs=[HBM] * 3,
        out_specs=(VMEM,) * 8,
        scratch_shapes=[pltpu.SMEM((6,), F32), pltpu.SemaphoreType.DMA((5,))],
        compiler_params=PARAMS,
        name="load",
    )(diffusivity, state, coarse_map)


def prep_kernel(consts_ref, order_ref, state_ref, entries_ref, cells_ref, packed_ref, drift_ref, pair_ref, cross_ref, strips_ref):
    piece = lambda f, t: state_ref[f, :, 128 * t : 128 * t + 128]
    odd = jnp.broadcast_to(const(consts_ref, 1), (64, 128)) > 0.5
    right, left = messages(piece, 64)
    pair_ref[0:64, :] = jnp.where(odd, left, right)
    cross_ref[0:64, :] = jnp.where(odd, right, left)
    put_strips(strips_ref, 0, piece, 64)
    ordered = split_dot(state_ref[...].reshape(384, 512), order_ref[...])
    for f in range(6):
        for k in range(4):
            cells_ref[f, k] = ordered[64 * f : 64 * f + 64, 128 * k : 128 * k + 128]
    means = block_means(lambda f, k, r: cells_ref[f, k, pl.ds(r, 16, stride=4), :], False)
    later = jnp.broadcast_to(const(consts_ref, 14), (16, 128)) > 0.5
    for f in range(6):
        terms = [entries_ref[6 * f + g] * means[g] for g in range(6)]
        total = (terms[0] + terms[1]) + (terms[2] + terms[3]) + (terms[4] + terms[5])
        drift_ref[f] = jnp.where(later, total, F32(0.0))
    for f in range(6):
        for j in range(3):
            put_pair(packed_ref, 3 * f + j, entries_ref[6 * f + j], entries_ref[6 * f + j + 3])


def block_means(load, inner):
    means = []
    for f in range(6):
        total = jnp.zeros((16, 128), F32)
        for k in range(4):
            total = total + ((load(f, k, 0) + load(f, k, 1)) + (load(f, k, 2) + load(f, k, 3)))
        if inner:
            lane = lanes((16, 128))
            total = jnp.where((lane > 0) & (lane < 127), total, F32(0.0))
        means.append(total * F32(1.0 / 16.0))
    return means


def prep(consts, order, state, entries):
    shape = lambda *dims: jax.ShapeDtypeStruct(dims, F32)
    return pl.pallas_call(
        prep_kernel,
        out_shape=(
            shape(6, 4, 64, 128),
            shape(32 * SLOT, 128),
            shape(6, 16, 128),
            shape(72, 128),
            shape(72, 128),
            shape(3, 72, 128),
        ),
        in_specs=[VMEM] * 4,
        out_specs=(VMEM,) * 6,
        compiler_params=PARAMS,
        cost_estimate=pl.CostEstimate(flops=4_000_000, bytes_accessed=2_000_000, transcendentals=0),
        name="prep",
    )(consts, order, state, entries)


def const(consts_ref, r):
    return consts_ref[pl.ds(r, 1), :]


def strips_above_below(consts_ref, pair_rows_ref, cross_rows_ref):
    odd = jnp.broadcast_to(const(consts_ref, 0), (4, 128)) > 0.5
    pick = lambda a, b: lambda f, t: jnp.where(
        odd, a[f, :, 128 * t : 128 * t + 128], b[f, :, 128 * t : 128 * t + 128]
    )
    return pick(pair_rows_ref, cross_rows_ref), pick(cross_rows_ref, pair_rows_ref)


def corners_kernel(consts_ref, pair_rows_ref, cross_rows_ref, pair_in, cross_in, pair_ref, cross_ref):
    del pair_in, cross_in
    odd = jnp.broadcast_to(const(consts_ref, 1), (4, 128)) > 0.5
    above, below = strips_above_below(consts_ref, pair_rows_ref, cross_rows_ref)
    for at, piece in ((64, below), (68, above)):
        right, left = messages(piece, 4)
        pair_ref[at : at + 4, :] = jnp.where(odd, left, right)
        cross_ref[at : at + 4, :] = jnp.where(odd, right, left)


def corners(consts, pair_rows, cross_rows, pair_columns, cross_columns):
    out = jax.ShapeDtypeStruct((72, 128), F32)
    return pl.pallas_call(
        corners_kernel,
        out_shape=(out, out),
        in_specs=[VMEM] * 5,
        out_specs=(VMEM, VMEM),
        input_output_aliases={3: 0, 4: 1},
        compiler_params=PARAMS,
        name="corners",
    )(consts, pair_rows, cross_rows, pair_columns, cross_columns)


def halo_exists(consts_ref):
    full = lambda r: jnp.broadcast_to(const(consts_ref, r), (8, 128))
    return jnp.where(lax.broadcasted_iota(jnp.int32, (8, 128), 0) < 4, full(3), full(2)) > 0.5


def middle_kernel(consts_ref, weights_ref, order_ref, cells_ref, drift_ref, pair_rows_ref, cross_rows_ref,
                  packed_in, strips_in, fine_ref, packed_ref, strips_ref, own_ref, buffer, face, halo, flat):
    del packed_in, strips_in
    above, below = strips_above_below(consts_ref, pair_rows_ref, cross_rows_ref)
    for f in range(6):
        for t in range(4):
            halo[8 * f : 8 * f + 4, 128 * t : 128 * t + 128] = below(f, t)
            halo[8 * f + 4 : 8 * f + 8, 128 * t : 128 * t + 128] = above(f, t)
    put_strips(strips_ref, 64, below, 4)
    put_strips(strips_ref, 68, above, 4)
    ordered = split_dot(halo[...], order_ref[...])
    for f in range(6):
        for k in range(4):
            buffer[0, f, k, TOP : TOP + 64, :] = cells_ref[f, k]
            piece = ordered[8 * f : 8 * f + 8, 128 * k : 128 * k + 128]
            buffer[0, f, k, TOP + 64 : TOP + 72, :] = piece
            buffer[0, f, k, TOP - 1 : TOP, :] = piece[7:8]
            buffer[0, f, k, TOP + 72 : TOP + 73, :] = cells_ref[f, k, 0:1, :]
    exists = halo_exists(consts_ref)

    def step_cells(now, later, tiles, last):
        for i in tiles:
            rows = pl.ds(8 * i, 8)
            speed = [FACE * jnp.tanh(buffer[now, 1, k, rows, :]) for k in range(4)]
            face[0, rows, :] = speed[0] + pltpu.roll(speed[3], 1, 1)
            for k in range(4):
                face[k + 1, rows, :] = speed[k] + (speed[k + 1] if k < 3 else pltpu.roll(speed[0], 127, 1))
            for k in range(4):
                face[5 + k, rows, :] = face[k, rows, :] - face[k + 1, rows, :]
        for f in range(6):
            rate = jnp.broadcast_to(const(consts_ref, 8 + f), (8, 128))
            keep = 1.0 - 4.0 * rate
            for i in tiles:
                rows = pl.ds(8 * i, 8)
                center = [buffer[now, f, k, rows, :] for k in range(4)]
                east = center[1:] + [pltpu.roll(center[0], 127, 1)]
                west = [pltpu.roll(center[3], 1, 1)] + center[:3]
                up, down = rate * weights_ref[0, rows, :], rate * weights_ref[1, rows, :]
                for k in range(4):
                    north = buffer[now, f, k, pl.ds(8 * i + 1, 8), :]
                    south = buffer[now, f, k, pl.ds(8 * i - 1, 8), :]
                    new = (up * north + down * south) + (
                        (east[k] * (rate - face[k + 1, rows, :]) + west[k] * (rate + face[k, rows, :]))
                        + center[k] * (keep + face[5 + k, rows, :])
                    )
                    if i == 9:
                        new = jnp.where(exists, new, F32(0.0))
                        buffer[later, f, k, TOP - 1 : TOP, :] = new[7:8]
                    if i == 1 and not last:
                        buffer[later, f, k, TOP + 72 : TOP + 73, :] = new[0:1]
                    buffer[later, f, k, rows, :] = new
                    if last:
                        at = 64 * f + 8 * i - TOP
                        flat[at : at + 8, 128 * k : 128 * k + 128] = new

    for step in range(FSTEPS):
        last = step == FSTEPS - 1
        step_cells(step % 2, (step + 1) % 2, range(1, 9) if last else range(1, 10), last)
    slot = FSTEPS % 2
    means = block_means(lambda f, k, r: buffer[slot, f, k, pl.ds(TOP + r, 16, stride=4), :], True)
    for j in range(3):
        put_pair(own_ref, j, means[j], means[j + 3], BACK)
        put_pair(packed_ref, 18 + j, means[j] - drift_ref[j], means[j + 3] - drift_ref[j + 3])
    fine_ref[...] = split_dot(flat[...], order_ref[...], transposed=True).reshape(6, 64, 512)


def middle(consts, weights, order, cells, drift, pair_rows, cross_rows, packed, strips):
    return pl.pallas_call(
        middle_kernel,
        out_shape=(
            jax.ShapeDtypeStruct((6, 64, 512), F32),
            jax.ShapeDtypeStruct((32 * SLOT, 128), F32),
            jax.ShapeDtypeStruct((3, 72, 128), F32),
            jax.ShapeDtypeStruct((32 * BACK, 128), F32),
        ),
        in_specs=[VMEM] * 9,
        out_specs=(VMEM,) * 4,
        scratch_shapes=[
            pltpu.VMEM((2, 6, 4, BUF, 128), F32),
            pltpu.VMEM((9, BUF, 128), F32),
            pltpu.VMEM((48, 512), F32),
            pltpu.VMEM((384, 512), F32),
        ],
        input_output_aliases={7: 1, 8: 2},
        compiler_params=PARAMS,
        cost_estimate=pl.CostEstimate(flops=20_000_000, bytes_accessed=4_000_000, transcendentals=200_000),
        name="middle",
    )(consts, weights, order, cells, drift, pair_rows, cross_rows, packed, strips)


def sides_kernel(consts_ref, weights_ref, spread_ref, strips_ref, pair_ref, cross_ref, packed_in, own_in,
                 edge_ref, packed_ref, own_ref, buffer):
    full = lambda r, count=8: jnp.broadcast_to(const(consts_ref, r), (count, 128))
    at = lanes((72, 128)) % 32
    odd = full(1, 72) > 0.5
    pair, cross = pair_ref[...], cross_ref[...]
    from_left, from_right = jnp.where(odd, pair, cross), jnp.where(odd, cross, pair)
    for tile in (2, 1, 0):
        value = jnp.where(at < 4, moved(from_left, -4 * tile), strips_ref[tile])
        value = jnp.where((at >= 24) & (at < 28), moved(from_right, 4 * tile), value)
        buffer[0, tile, TOP : TOP + 72, :] = value
        buffer[0, tile, TOP - 1 : TOP, :] = value[71:72]
        buffer[0, tile, TOP + 72 : TOP + 73, :] = value[0:1]
    exists, inside = halo_exists(consts_ref), full(4) > 0.5
    rates = [full(5 + tile) for tile in range(3)]
    keeps = [1.0 - 4.0 * rate for rate in rates]
    for step in range(FSTEPS):
        now, later = step % 2, (step + 1) % 2
        last = step == FSTEPS - 1
        for i in range(1, 9) if last else range(1, 10):
            rows = pl.ds(8 * i, 8)
            up, down = weights_ref[0, rows, :], weights_ref[1, rows, :]
            center = [buffer[now, tile, rows, :] for tile in range(3)]
            east = [pltpu.roll(c, 127, 1) for c in center]
            west = [pltpu.roll(c, 1, 1) for c in center]
            speed = jnp.tanh(center[2])
            fe, fw = FACE * (speed + jnp.tanh(east[2])), FACE * (speed + jnp.tanh(west[2]))
            for tile in range(2 if last else 3):
                rate = rates[tile]
                north = buffer[now, tile, pl.ds(8 * i + 1, 8), :]
                south = buffer[now, tile, pl.ds(8 * i - 1, 8), :]
                new = rate * (up * north + down * south) + (
                    (east[tile] * (rate - fe) + west[tile] * (rate + fw)) + center[tile] * (keeps[tile] + (fw - fe))
                )
                if i == 9:
                    new = jnp.where(exists, new, F32(0.0))
                new = jnp.where(inside, new, F32(0.0))
                if i == 9:
                    buffer[later, tile, TOP - 1 : TOP, :] = new[7:8]
                if i == 1 and not last:
                    buffer[later, tile, TOP + 72 : TOP + 73, :] = new[0:1]
                buffer[later, tile, rows, :] = new
                if last:
                    edge_ref[tile, 8 * i - TOP : 8 * i - TOP + 8, :] = new
    slot = FSTEPS % 2
    sums = []
    for tile in range(2):
        load = lambda r: buffer[slot, tile, pl.ds(TOP + r, 16, stride=4), :]
        sums.append((load(0) + load(1)) + (load(2) + load(3)))
    own = split_dot(jnp.concatenate(sums, axis=1), spread_ref[...])
    left = lanes((16, 128)) % 64 == 0
    for j in range(3):
        piece = own[:, 128 * j : 128 * j + 128]
        pieces = jnp.where(left, piece, F32(0.0)), jnp.where(left, F32(0.0), piece)
        for half in range(2):
            rows = pl.ds(SLOT * half + 18 + j, 16, stride=2 * SLOT)
            packed_ref[rows, :] = packed_in[rows, :] + pieces[half]
            rows = pl.ds(BACK * half + j, 16, stride=2 * BACK)
            own_ref[rows, :] = own_in[rows, :] + pieces[half]


def sides(consts, weights, spread, strips, pair_columns, cross_columns, packed, own):
    return pl.pallas_call(
        sides_kernel,
        out_shape=(
            jax.ShapeDtypeStruct((2, 64, 128), F32),
            jax.ShapeDtypeStruct((32 * SLOT, 128), F32),
            jax.ShapeDtypeStruct((32 * BACK, 128), F32),
        ),
        in_specs=[VMEM] * 8,
        out_specs=(VMEM,) * 3,
        scratch_shapes=[pltpu.VMEM((2, 3, BUF, 128), F32)],
        input_output_aliases={6: 1, 7: 2},
        compiler_params=PARAMS,
        name="sides",
    )(consts, weights, spread, strips, pair_columns, cross_columns, packed, own)


def scan_kernel(slices, packed_ref, mapped_ref, other, rows):
    other[...] = pltpu.roll(packed_ref[...], 64, 1)
    carry = [jnp.zeros((1, 128), F32)] * 6
    for n in range(slices):
        base = SLOT * n
        line = lambda k, half: (other if half else packed_ref)[pl.ds(base + k, 1), :]
        mapped = []
        for f in range(6):
            terms = [line(3 * f + g % 3, g >= 3) * carry[g] for g in range(6)]
            total = (terms[0] + terms[1]) + (terms[2] + terms[3]) + (terms[4] + terms[5])
            mapped.append(total + line(18 + f % 3, f >= 3))
            rows[f, pl.ds(n, 1), :] = mapped[f]
        carry = mapped
    left = lanes((slices, 128)) < 64
    for j in range(3):
        mapped_ref[pl.ds(j, slices, stride=BACK), :] = jnp.where(left, rows[j], pltpu.roll(rows[j + 3], 64, 1))


def scanned(packed, slices):
    return pl.pallas_call(
        functools.partial(scan_kernel, slices),
        out_shape=jax.ShapeDtypeStruct((BACK * slices, 128), F32),
        in_specs=[VMEM],
        out_specs=VMEM,
        scratch_shapes=[pltpu.VMEM((SLOT * slices, 128), F32), pltpu.VMEM((6, slices, 128), F32)],
        compiler_params=PARAMS,
        name="scan",
    )(packed)


def final_kernel(fine_ref, edge_ref, own_ref, mapped_ref, out_ref, wide, done, sems):
    left = lanes((16, 128)) < 64
    upper = lax.broadcasted_iota(jnp.int32, (8, 128), 0) < 4
    lane = lanes((8, 128))
    for f in range(6):
        j = f % 3
        rows = pl.ds(j, 16, stride=2 * BACK), pl.ds(BACK + j, 16, stride=2 * BACK)
        even, odd = (mapped_ref[r, :] - own_ref[r, :] for r in rows)
        if f < 3:
            cells = jnp.where(left, even, pltpu.roll(odd, 64, 1))
        else:
            cells = jnp.where(left, pltpu.roll(even, 64, 1), odd)
        for t in range(4):
            source = 32 * t + lanes((16, 128)) // 4
            wide[f, t] = jnp.take_along_axis(cells, source, axis=1)
    copies = []
    for f in range(6):
        tile, base = f // 4, 32 * (f % 4)
        for t in range(4):
            cut = slice(128 * t, 128 * t + 128)
            for q in range(8):
                first = jnp.broadcast_to(wide[f, t, pl.ds(2 * q, 1), :], (8, 128))
                second = jnp.broadcast_to(wide[f, t, pl.ds(2 * q + 1, 1), :], (8, 128))
                rows = slice(8 * q, 8 * q + 8)
                own = fine_ref[f, rows, cut]
                if t == 0:
                    own = jnp.where(lane < 4, moved(edge_ref[tile, rows, :], -(base + 4)), own)
                if t == 3:
                    own = jnp.where(lane >= 124, moved(edge_ref[tile, rows, :], 104 - base), own)
                done[f, rows, cut] = own + jnp.where(upper, first, second)
        copies.append(pltpu.make_async_copy(done.at[f], out_ref.at[f], sems.at[f]))
        copies[f].start()
    for copy in copies:
        copy.wait()


def final(fine_state, edge, own, mapped):
    return pl.pallas_call(
        final_kernel,
        out_shape=jax.ShapeDtypeStruct((6, 64, 512), F32),
        in_specs=[VMEM] * 4,
        out_specs=HBM,
        scratch_shapes=[
            pltpu.VMEM((6, 4, 16, 128), F32),
            pltpu.VMEM((6, 64, 512), F32),
            pltpu.SemaphoreType.DMA((6,)),
        ],
        compiler_params=PARAMS,
        name="final",
    )(fine_state, edge, own, mapped)


def swapped(pair, cross, axis):
    size = lax.axis_size(axis)
    couples = lambda first: [(i, i + 1) for i in range(first, size - 1, 2)]
    both = lambda links: links + [(b, a) for a, b in links]
    return lax.ppermute(pair, axis, both(couples(0))), lax.ppermute(cross, axis, both(couples(1)))


def local(starts, coarse_map, diffusivity):
    in_hbm = lambda x: pltpu.with_memory_space_constraint(x, pltpu.HBM)
    slices = lax.axis_size("tm")
    state, entries, pair_rows, cross_rows, consts, weights, order, spread = load(
        in_hbm(diffusivity), in_hbm(starts[0]), in_hbm(coarse_map[0])
    )
    pair_rows, cross_rows = swapped(pair_rows, cross_rows, "row")
    cells, packed, drift, pair_columns, cross_columns, strips = prep(consts, order, state, entries)
    pair_columns, cross_columns = corners(consts, pair_rows, cross_rows, pair_columns, cross_columns)
    pair_columns, cross_columns = swapped(pair_columns, cross_columns, "gz")
    fine_state, packed, strips, own = middle(
        consts, weights, order, cells, drift, pair_rows, cross_rows, packed, strips
    )
    edge, packed, own = sides(consts, weights, spread, strips, pair_columns, cross_columns, packed, own)
    slots = packed.reshape(slices, 1, SLOT * 128)
    packed = lax.all_to_all(slots, "tm", 0, 0, tiled=True).reshape(packed.shape)
    mapped = scanned(packed, slices)
    slots = mapped.reshape(slices, 1, BACK * 128)
    mapped = lax.all_to_all(slots, "tm", 0, 0, tiled=True).reshape(mapped.shape)
    return final(fine_state, edge, own, mapped)[None]


def solution(mesh):
    placed = (P("tm", None, "row", "gz"), P("tm", None, "row", "gz"), P())
    return jax.shard_map(
        local, mesh=mesh, in_specs=placed, out_specs=P("tm", None, "row", "gz"), check_vma=False
    )
```

```python
import functools

import jax
import jax.numpy as jnp
from jax import lax
from jax.experimental import pallas as pl
from jax.experimental.pallas import tpu as pltpu
from jax.sharding import PartitionSpec as P


FSTEPS = 4
STEP = 0.24
FACE = 0.24 * 0.25 * 0.25
F32, BF16 = jnp.float32, jnp.bfloat16
TOP = 8
BUF = 88
PARAMS = pltpu.CompilerParams(vmem_limit_bytes=24 << 20)
VMEM = pl.BlockSpec(memory_space=pltpu.VMEM)
SMEM = pl.BlockSpec(memory_space=pltpu.SMEM)
HBM = pl.BlockSpec(memory_space=pltpu.HBM)


def lanes(shape):
    return lax.broadcasted_iota(jnp.int32, shape, len(shape) - 1)


SLOT, BACK = 21, 3


def put_pair(packed_ref, k, low, high, height=SLOT):
    left = lanes(low.shape) < 64
    packed_ref[pl.ds(k, 16, stride=2 * height), :] = jnp.where(left, low, pltpu.roll(high, 64, 1))
    packed_ref[pl.ds(height + k, 16, stride=2 * height), :] = jnp.where(left, pltpu.roll(low, 64, 1), high)


def split_dot(x, matrix, transposed=False):
    high = x.astype(BF16)
    low = (x - high.astype(F32)).astype(BF16)
    dims = (((1,), (1 if transposed else 0,)), ((), ()))
    dot = lambda part: lax.dot_general(part, matrix, dims, preferred_element_type=F32)
    return dot(high) + dot(low)


PLACES = [(0, q, q) for q in range(4)] + [(1, q, 4 + q) for q in range(2)] + [(2, q, 1) for q in range(4)]


def moved(x, shift):
    shift = shift % 128
    return pltpu.roll(x, shift, 1) if shift else x


def messages(column, count):
    lane = lanes((count, 128))
    right, left = jnp.zeros((count, 128), F32), jnp.zeros((count, 128), F32)
    for tile, q, f in PLACES:
        at = 32 * q + 4 * tile
        right = jnp.where((lane >= at) & (lane < at + 4), moved(column(f, 3), at + 4), right)
        at = 32 * q + 24 - 4 * tile
        left = jnp.where((lane >= at) & (lane < at + 4), moved(column(f, 0), at), left)
    return right, left


def put_strips(strips_ref, rows, column, count):
    lane = lanes((count, 128))
    for tile in range(3):
        total = jnp.zeros((count, 128), F32)
        for other, q, f in PLACES:
            if other == tile:
                at = 32 * q
                total = jnp.where((lane >= at + 4) & (lane < at + 12), moved(column(f, 0), at + 4), total)
                total = jnp.where((lane >= at + 16) & (lane < at + 24), moved(column(f, 3), at + 24), total)
        strips_ref[tile, rows : rows + count, :] = total


def load_kernel(nu_hbm, starts_ref, map_ref, state_ref, entries_ref, pair_ref, cross_ref, consts_ref, weights_ref, order_ref,
                spread_ref, nu_ref, sems):
    outer = [pl.ds(0, 8), pl.ds(56, 8), pl.ds(8, 48)]
    copies = [pltpu.make_async_copy(starts_ref.at[:, r, :], state_ref.at[:, r, :], sems.at[i]) for i, r in enumerate(outer)]
    copies.append(pltpu.make_async_copy(nu_hbm, nu_ref, sems.at[3]))
    copies.append(pltpu.make_async_copy(map_ref, entries_ref, sems.at[4]))
    for copy in copies:
        copy.start()
    row, column = lax.axis_index("row"), lax.axis_index("gz")
    for t in range(4):
        z = lax.broadcasted_iota(jnp.int32, (128, 512), 0) + 128 * t
        place = lax.broadcasted_iota(jnp.int32, (128, 512), 1)
        order_ref[128 * t : 128 * t + 128, :] = jnp.where(128 * (z % 4) + z // 4 == place, F32(1), F32(0)).astype(BF16)
    lane = lax.broadcasted_iota(jnp.int32, (256, 384), 0)
    target = lax.broadcasted_iota(jnp.int32, (256, 384), 1)
    field, at = lane // 32, lane % 32
    base = jnp.where(field < 3, 128 * field, 128 * (field - 3) + 64)
    to = jnp.where((at >= 4) & (at < 8), base, jnp.where((at >= 20) & (at < 24), base + 63, -1))
    to = jnp.where(field < 6, to, -1)
    spread_ref[...] = jnp.where(to == target, F32(1.0 / 16.0), F32(0.0)).astype(BF16)
    line = lax.broadcasted_iota(jnp.int32, (BUF, 128), 0)
    radius = (jnp.where(line >= TOP + 68, line - (TOP + 72), line - TOP) + row * 64).astype(F32)
    weights_ref[0] = (radius + 1.0) / (radius + 0.5)
    weights_ref[1] = radius / (radius + 0.5)
    copies[3].wait()
    line, lane = lax.broadcasted_iota(jnp.int32, (16, 128), 0), lanes((16, 128))
    flag = lambda condition: jnp.where(condition, F32(1.0), F32(0.0))
    group, at = lane // 32, lane % 32
    low, high = jnp.where(column > 0, 0, 4), jnp.where(column < 3, 32, 24)
    rates = lambda fields: functools.reduce(
        lambda a, q: jnp.where(group == q, STEP * nu_ref[fields[q]], a), range(4), jnp.zeros((16, 128), F32)
    )
    values = [flag(row % 2 == 1), flag(column % 2 == 1), flag(row > 0), flag(row < 3)]
    values += [flag((at >= low) & (at < high)), rates((0, 1, 2, 3)), rates((4, 5, 5, 5)), rates((1, 1, 1, 1))]
    values += [rates((f, f, f, f)) for f in range(6)]
    values += [flag(lax.axis_index("tm") > 0)]
    total = jnp.zeros((16, 128), F32)
    for r, value in enumerate(values):
        total = jnp.where(line == r, value, total)
    consts_ref[...] = total
    copies[0].wait()
    copies[1].wait()
    odd = row % 2 == 1
    for f in range(6):
        first, last = state_ref[f, 0:4, :], state_ref[f, 60:64, :]
        pair_ref[f] = jnp.where(odd, first, last)
        cross_ref[f] = jnp.where(odd, last, first)
    copies[2].wait()
    copies[4].wait()


def load(diffusivity, state, coarse_map):
    shape = lambda *dims: jax.ShapeDtypeStruct(dims, F32)
    return pl.pallas_call(
        load_kernel,
        out_shape=(
            shape(6, 64, 512),
            shape(36, 16, 128),
            shape(6, 4, 512),
            shape(6, 4, 512),
            shape(16, 128),
            shape(2, BUF, 128),
            jax.ShapeDtypeStruct((512, 512), BF16),
            jax.ShapeDtypeStruct((256, 384), BF16),
        ),
        in_specs=[HBM] * 3,
        out_specs=(VMEM,) * 8,
        scratch_shapes=[pltpu.SMEM((6,), F32), pltpu.SemaphoreType.DMA((5,))],
        compiler_params=PARAMS,
        name="load",
    )(diffusivity, state, coarse_map)


def prep_kernel(consts_ref, order_ref, state_ref, entries_ref, cells_ref, packed_ref, drift_ref, pair_ref, cross_ref, strips_ref):
    piece = lambda f, t: state_ref[f, :, 128 * t : 128 * t + 128]
    odd = jnp.broadcast_to(const(consts_ref, 1), (64, 128)) > 0.5
    right, left = messages(piece, 64)
    pair_ref[0:64, :] = jnp.where(odd, left, right)
    cross_ref[0:64, :] = jnp.where(odd, right, left)
    put_strips(strips_ref, 0, piece, 64)
    ordered = split_dot(state_ref[...].reshape(384, 512), order_ref[...])
    for f in range(6):
        for k in range(4):
            cells_ref[f, k] = ordered[64 * f : 64 * f + 64, 128 * k : 128 * k + 128]
    means = block_means(lambda f, k, r: cells_ref[f, k, pl.ds(r, 16, stride=4), :], False)
    later = jnp.broadcast_to(const(consts_ref, 14), (16, 128)) > 0.5
    for f in range(6):
        terms = [entries_ref[6 * f + g] * means[g] for g in range(6)]
        total = (terms[0] + terms[1]) + (terms[2] + terms[3]) + (terms[4] + terms[5])
        drift_ref[f] = jnp.where(later, total, F32(0.0))
    for f in range(6):
        for j in range(3):
            put_pair(packed_ref, 3 * f + j, entries_ref[6 * f + j], entries_ref[6 * f + j + 3])


def block_means(load, inner):
    means = []
    for f in range(6):
        total = jnp.zeros((16, 128), F32)
        for k in range(4):
            total = total + ((load(f, k, 0) + load(f, k, 1)) + (load(f, k, 2) + load(f, k, 3)))
        if inner:
            lane = lanes((16, 128))
            total = jnp.where((lane > 0) & (lane < 127), total, F32(0.0))
        means.append(total * F32(1.0 / 16.0))
    return means


def prep(consts, order, state, entries):
    shape = lambda *dims: jax.ShapeDtypeStruct(dims, F32)
    return pl.pallas_call(
        prep_kernel,
        out_shape=(
            shape(6, 4, 64, 128),
            shape(32 * SLOT, 128),
            shape(6, 16, 128),
            shape(72, 128),
            shape(72, 128),
            shape(3, 72, 128),
        ),
        in_specs=[VMEM] * 4,
        out_specs=(VMEM,) * 6,
        compiler_params=PARAMS,
        cost_estimate=pl.CostEstimate(flops=4_000_000, bytes_accessed=2_000_000, transcendentals=0),
        name="prep",
    )(consts, order, state, entries)


def const(consts_ref, r):
    return consts_ref[pl.ds(r, 1), :]


def strips_above_below(consts_ref, pair_rows_ref, cross_rows_ref):
    odd = jnp.broadcast_to(const(consts_ref, 0), (4, 128)) > 0.5
    pick = lambda a, b: lambda f, t: jnp.where(
        odd, a[f, :, 128 * t : 128 * t + 128], b[f, :, 128 * t : 128 * t + 128]
    )
    return pick(pair_rows_ref, cross_rows_ref), pick(cross_rows_ref, pair_rows_ref)


def corners_kernel(consts_ref, pair_rows_ref, cross_rows_ref, pair_in, cross_in, pair_ref, cross_ref):
    del pair_in, cross_in
    odd = jnp.broadcast_to(const(consts_ref, 1), (4, 128)) > 0.5
    above, below = strips_above_below(consts_ref, pair_rows_ref, cross_rows_ref)
    for at, piece in ((64, below), (68, above)):
        right, left = messages(piece, 4)
        pair_ref[at : at + 4, :] = jnp.where(odd, left, right)
        cross_ref[at : at + 4, :] = jnp.where(odd, right, left)


def corners(consts, pair_rows, cross_rows, pair_columns, cross_columns):
    out = jax.ShapeDtypeStruct((72, 128), F32)
    return pl.pallas_call(
        corners_kernel,
        out_shape=(out, out),
        in_specs=[VMEM] * 5,
        out_specs=(VMEM, VMEM),
        input_output_aliases={3: 0, 4: 1},
        compiler_params=PARAMS,
        name="corners",
    )(consts, pair_rows, cross_rows, pair_columns, cross_columns)


def halo_exists(consts_ref):
    full = lambda r: jnp.broadcast_to(const(consts_ref, r), (8, 128))
    return jnp.where(lax.broadcasted_iota(jnp.int32, (8, 128), 0) < 4, full(3), full(2)) > 0.5


def middle_kernel(consts_ref, weights_ref, order_ref, cells_ref, drift_ref, pair_rows_ref, cross_rows_ref,
                  packed_in, strips_in, fine_ref, packed_ref, strips_ref, own_ref, buffer, face, halo, flat):
    del packed_in, strips_in
    above, below = strips_above_below(consts_ref, pair_rows_ref, cross_rows_ref)
    for f in range(6):
        for t in range(4):
            halo[8 * f : 8 * f + 4, 128 * t : 128 * t + 128] = below(f, t)
            halo[8 * f + 4 : 8 * f + 8, 128 * t : 128 * t + 128] = above(f, t)
    put_strips(strips_ref, 64, below, 4)
    put_strips(strips_ref, 68, above, 4)
    ordered = split_dot(halo[...], order_ref[...])
    for f in range(6):
        for k in range(4):
            buffer[0, f, k, TOP : TOP + 64, :] = cells_ref[f, k]
            piece = ordered[8 * f : 8 * f + 8, 128 * k : 128 * k + 128]
            buffer[0, f, k, TOP + 64 : TOP + 72, :] = piece
            buffer[0, f, k, TOP - 1 : TOP, :] = piece[7:8]
            buffer[0, f, k, TOP + 72 : TOP + 73, :] = cells_ref[f, k, 0:1, :]
    exists = halo_exists(consts_ref)

    def step_cells(now, later, tiles, last):
        for i in tiles:
            rows = pl.ds(8 * i, 8)
            speed = [FACE * jnp.tanh(buffer[now, 1, k, rows, :]) for k in range(4)]
            face[0, rows, :] = speed[0] + pltpu.roll(speed[3], 1, 1)
            for k in range(4):
                face[k + 1, rows, :] = speed[k] + (speed[k + 1] if k < 3 else pltpu.roll(speed[0], 127, 1))
            for k in range(4):
                face[5 + k, rows, :] = face[k, rows, :] - face[k + 1, rows, :]
        for f in range(6):
            rate = jnp.broadcast_to(const(consts_ref, 8 + f), (8, 128))
            keep = 1.0 - 4.0 * rate
            for i in tiles:
                rows = pl.ds(8 * i, 8)
                center = [buffer[now, f, k, rows, :] for k in range(4)]
                east = center[1:] + [pltpu.roll(center[0], 127, 1)]
                west = [pltpu.roll(center[3], 1, 1)] + center[:3]
                up, down = rate * weights_ref[0, rows, :], rate * weights_ref[1, rows, :]
                for k in range(4):
                    north = buffer[now, f, k, pl.ds(8 * i + 1, 8), :]
                    south = buffer[now, f, k, pl.ds(8 * i - 1, 8), :]
                    new = (up * north + down * south) + (
                        (east[k] * (rate - face[k + 1, rows, :]) + west[k] * (rate + face[k, rows, :]))
                        + center[k] * (keep + face[5 + k, rows, :])
                    )
                    if i == 9:
                        new = jnp.where(exists, new, F32(0.0))
                        buffer[later, f, k, TOP - 1 : TOP, :] = new[7:8]
                    if i == 1 and not last:
                        buffer[later, f, k, TOP + 72 : TOP + 73, :] = new[0:1]
                    buffer[later, f, k, rows, :] = new
                    if last:
                        at = 64 * f + 8 * i - TOP
                        flat[at : at + 8, 128 * k : 128 * k + 128] = new

    for step in range(FSTEPS):
        last = step == FSTEPS - 1
        step_cells(step % 2, (step + 1) % 2, range(1, 9) if last else range(1, 10), last)
    slot = FSTEPS % 2
    means = block_means(lambda f, k, r: buffer[slot, f, k, pl.ds(TOP + r, 16, stride=4), :], True)
    for j in range(3):
        put_pair(own_ref, j, means[j], means[j + 3], BACK)
        put_pair(packed_ref, 18 + j, means[j] - drift_ref[j], means[j + 3] - drift_ref[j + 3])
    fine_ref[...] = split_dot(flat[...], order_ref[...], transposed=True).reshape(6, 64, 512)


def middle(consts, weights, order, cells, drift, pair_rows, cross_rows, packed, strips):
    return pl.pallas_call(
        middle_kernel,
        out_shape=(
            jax.ShapeDtypeStruct((6, 64, 512), F32),
            jax.ShapeDtypeStruct((32 * SLOT, 128), F32),
            jax.ShapeDtypeStruct((3, 72, 128), F32),
            jax.ShapeDtypeStruct((32 * BACK, 128), F32),
        ),
        in_specs=[VMEM] * 9,
        out_specs=(VMEM,) * 4,
        scratch_shapes=[
            pltpu.VMEM((2, 6, 4, BUF, 128), F32),
            pltpu.VMEM((9, BUF, 128), F32),
            pltpu.VMEM((48, 512), F32),
            pltpu.VMEM((384, 512), F32),
        ],
        input_output_aliases={7: 1, 8: 2},
        compiler_params=PARAMS,
        cost_estimate=pl.CostEstimate(flops=20_000_000, bytes_accessed=4_000_000, transcendentals=200_000),
        name="middle",
    )(consts, weights, order, cells, drift, pair_rows, cross_rows, packed, strips)


def sides_kernel(consts_ref, weights_ref, spread_ref, strips_ref, pair_ref, cross_ref, packed_in, own_in,
                 edge_ref, packed_ref, own_ref, buffer):
    full = lambda r, count=8: jnp.broadcast_to(const(consts_ref, r), (count, 128))
    at = lanes((72, 128)) % 32
    odd = full(1, 72) > 0.5
    pair, cross = pair_ref[...], cross_ref[...]
    from_left, from_right = jnp.where(odd, pair, cross), jnp.where(odd, cross, pair)
    for tile in (2, 1, 0):
        value = jnp.where(at < 4, moved(from_left, -4 * tile), strips_ref[tile])
        value = jnp.where((at >= 24) & (at < 28), moved(from_right, 4 * tile), value)
        buffer[0, tile, TOP : TOP + 72, :] = value
        buffer[0, tile, TOP - 1 : TOP, :] = value[71:72]
        buffer[0, tile, TOP + 72 : TOP + 73, :] = value[0:1]
    exists, inside = halo_exists(consts_ref), full(4) > 0.5
    rates = [full(5 + tile) for tile in range(3)]
    keeps = [1.0 - 4.0 * rate for rate in rates]
    for step in range(FSTEPS):
        now, later = step % 2, (step + 1) % 2
        last = step == FSTEPS - 1
        for i in range(1, 9) if last else range(1, 10):
            rows = pl.ds(8 * i, 8)
            up, down = weights_ref[0, rows, :], weights_ref[1, rows, :]
            center = [buffer[now, tile, rows, :] for tile in range(3)]
            east = [pltpu.roll(c, 127, 1) for c in center]
            west = [pltpu.roll(c, 1, 1) for c in center]
            speed = jnp.tanh(center[2])
            fe, fw = FACE * (speed + jnp.tanh(east[2])), FACE * (speed + jnp.tanh(west[2]))
            for tile in range(2 if last else 3):
                rate = rates[tile]
                north = buffer[now, tile, pl.ds(8 * i + 1, 8), :]
                south = buffer[now, tile, pl.ds(8 * i - 1, 8), :]
                new = rate * (up * north + down * south) + (
                    (east[tile] * (rate - fe) + west[tile] * (rate + fw)) + center[tile] * (keeps[tile] + (fw - fe))
                )
                if i == 9:
                    new = jnp.where(exists, new, F32(0.0))
                new = jnp.where(inside, new, F32(0.0))
                if i == 9:
                    buffer[later, tile, TOP - 1 : TOP, :] = new[7:8]
                if i == 1 and not last:
                    buffer[later, tile, TOP + 72 : TOP + 73, :] = new[0:1]
                buffer[later, tile, rows, :] = new
                if last:
                    edge_ref[tile, 8 * i - TOP : 8 * i - TOP + 8, :] = new
    slot = FSTEPS % 2
    sums = []
    for tile in range(2):
        load = lambda r: buffer[slot, tile, pl.ds(TOP + r, 16, stride=4), :]
        sums.append((load(0) + load(1)) + (load(2) + load(3)))
    own = split_dot(jnp.concatenate(sums, axis=1), spread_ref[...])
    left = lanes((16, 128)) % 64 == 0
    for j in range(3):
        piece = own[:, 128 * j : 128 * j + 128]
        pieces = jnp.where(left, piece, F32(0.0)), jnp.where(left, F32(0.0), piece)
        for half in range(2):
            rows = pl.ds(SLOT * half + 18 + j, 16, stride=2 * SLOT)
            packed_ref[rows, :] = packed_in[rows, :] + pieces[half]
            rows = pl.ds(BACK * half + j, 16, stride=2 * BACK)
            own_ref[rows, :] = own_in[rows, :] + pieces[half]


def sides(consts, weights, spread, strips, pair_columns, cross_columns, packed, own):
    return pl.pallas_call(
        sides_kernel,
        out_shape=(
            jax.ShapeDtypeStruct((2, 64, 128), F32),
            jax.ShapeDtypeStruct((32 * SLOT, 128), F32),
            jax.ShapeDtypeStruct((32 * BACK, 128), F32),
        ),
        in_specs=[VMEM] * 8,
        out_specs=(VMEM,) * 3,
        scratch_shapes=[pltpu.VMEM((2, 3, BUF, 128), F32)],
        input_output_aliases={6: 1, 7: 2},
        compiler_params=PARAMS,
        name="sides",
    )(consts, weights, spread, strips, pair_columns, cross_columns, packed, own)


def scan_kernel(slices, packed_ref, mapped_ref, other, rows):
    other[...] = pltpu.roll(packed_ref[...], 64, 1)
    carry = [jnp.zeros((1, 128), F32)] * 6
    for n in range(slices):
        base = SLOT * n
        line = lambda k, half: (other if half else packed_ref)[pl.ds(base + k, 1), :]
        mapped = []
        for f in range(6):
            terms = [line(3 * f + g % 3, g >= 3) * carry[g] for g in range(6)]
            total = (terms[0] + terms[1]) + (terms[2] + terms[3]) + (terms[4] + terms[5])
            mapped.append(total + line(18 + f % 3, f >= 3))
            rows[f, pl.ds(n, 1), :] = mapped[f]
        carry = mapped
    left = lanes((slices, 128)) < 64
    for j in range(3):
        mapped_ref[pl.ds(j, slices, stride=BACK), :] = jnp.where(left, rows[j], pltpu.roll(rows[j + 3], 64, 1))


def scanned(packed, slices):
    return pl.pallas_call(
        functools.partial(scan_kernel, slices),
        out_shape=jax.ShapeDtypeStruct((BACK * slices, 128), F32),
        in_specs=[VMEM],
        out_specs=VMEM,
        scratch_shapes=[pltpu.VMEM((SLOT * slices, 128), F32), pltpu.VMEM((6, slices, 128), F32)],
        compiler_params=PARAMS,
        name="scan",
    )(packed)


def final_kernel(fine_ref, edge_ref, own_ref, mapped_ref, out_ref, wide, done, sems):
    left = lanes((16, 128)) < 64
    upper = lax.broadcasted_iota(jnp.int32, (8, 128), 0) < 4
    lane = lanes((8, 128))
    for f in range(6):
        j = f % 3
        rows = pl.ds(j, 16, stride=2 * BACK), pl.ds(BACK + j, 16, stride=2 * BACK)
        even, odd = (mapped_ref[r, :] - own_ref[r, :] for r in rows)
        if f < 3:
            cells = jnp.where(left, even, pltpu.roll(odd, 64, 1))
        else:
            cells = jnp.where(left, pltpu.roll(even, 64, 1), odd)
        for t in range(4):
            source = 32 * t + lanes((16, 128)) // 4
            wide[f, t] = jnp.take_along_axis(cells, source, axis=1)
    copies = []
    for f in range(6):
        tile, base = f // 4, 32 * (f % 4)
        for t in range(4):
            cut = slice(128 * t, 128 * t + 128)
            for q in range(8):
                first = jnp.broadcast_to(wide[f, t, pl.ds(2 * q, 1), :], (8, 128))
                second = jnp.broadcast_to(wide[f, t, pl.ds(2 * q + 1, 1), :], (8, 128))
                rows = slice(8 * q, 8 * q + 8)
                own = fine_ref[f, rows, cut]
                if t == 0:
                    own = jnp.where(lane < 4, moved(edge_ref[tile, rows, :], -(base + 4)), own)
                if t == 3:
                    own = jnp.where(lane >= 124, moved(edge_ref[tile, rows, :], 104 - base), own)
                done[f, rows, cut] = own + jnp.where(upper, first, second)
        copies.append(pltpu.make_async_copy(done.at[f], out_ref.at[f], sems.at[f]))
        copies[f].start()
    for copy in copies:
        copy.wait()


def final(fine_state, edge, own, mapped):
    return pl.pallas_call(
        final_kernel,
        out_shape=jax.ShapeDtypeStruct((6, 64, 512), F32),
        in_specs=[VMEM] * 4,
        out_specs=HBM,
        scratch_shapes=[
            pltpu.VMEM((6, 4, 16, 128), F32),
            pltpu.VMEM((6, 64, 512), F32),
            pltpu.SemaphoreType.DMA((6,)),
        ],
        compiler_params=PARAMS,
        name="final",
    )(fine_state, edge, own, mapped)


def swapped(pair, cross, axis):
    size = lax.axis_size(axis)
    couples = lambda first: [(i, i + 1) for i in range(first, size - 1, 2)]
    both = lambda links: links + [(b, a) for a, b in links]
    if axis == "gz":
        cross = lax.ppermute(cross, axis, both(couples(1)))
        return lax.ppermute(pair, axis, both(couples(0))), cross
    return lax.ppermute(pair, axis, both(couples(0))), lax.ppermute(cross, axis, both(couples(1)))


def whole(starts, coarse_map, diffusivity):
    in_hbm = lambda x: pltpu.with_memory_space_constraint(x, pltpu.HBM)
    slices = lax.axis_size("tm")
    state, entries, pair_rows, cross_rows, consts, weights, order, spread = load(
        in_hbm(diffusivity), in_hbm(starts[0]), in_hbm(coarse_map[0])
    )
    pair_rows, cross_rows = swapped(pair_rows, cross_rows, "row")
    cells, packed, drift, pair_columns, cross_columns, strips = prep(consts, order, state, entries)
    pair_columns, cross_columns = corners(consts, pair_rows, cross_rows, pair_columns, cross_columns)
    pair_columns, cross_columns = swapped(pair_columns, cross_columns, "gz")
    fine_state, packed, strips, own = middle(
        consts, weights, order, cells, drift, pair_rows, cross_rows, packed, strips
    )
    edge, packed, own = sides(consts, weights, spread, strips, pair_columns, cross_columns, packed, own)
    slots = packed.reshape(slices, 1, SLOT * 128)
    packed = lax.all_to_all(slots, "tm", 0, 0, tiled=True).reshape(packed.shape)
    mapped = scanned(packed, slices)
    slots = mapped.reshape(slices, 1, BACK * 128)
    mapped = lax.all_to_all(slots, "tm", 0, 0, tiled=True).reshape(mapped.shape)
    return final(fine_state, edge, own, mapped)[None]


def solution(mesh):
    placed = (P("tm", None, "row", "gz"), P("tm", None, "row", "gz"), P())
    return jax.shard_map(whole, mesh=mesh, in_specs=placed, out_specs=P("tm", None, "row", "gz"), check_vma=False)
```
